512 devices in a mesh: pixel: 4 (over y), crop: 8 (over z_lo, core), member: 16 (over x, z_hi).
Axes of the slice: x: 4, y: 4, z: 16 (z_hi: 4, z_lo: 4; z = z_hi * 4 + z_lo), core: 2. Of those that a mesh axis runs over, the one named last changes fastest.
Arguments:
- forcing: bfloat16 [52, 8, 12288], P(None, None, ('pixel', 'crop')), may hold values from -6 to 6
- observed: bfloat16 [52, 12288], P(None, ('pixel', 'crop')), may hold values from -6 to 6
- obs_sigma: float32 [12288], P(('pixel', 'crop')), may hold values from 0.5 to 2
- pixel_class: int32 [12288, 1], P(('pixel', 'crop')), may hold values from 0 to 63; in each aligned block of 384 rows (0 to 383, 384 to 767, ...) at most 8 rows name the same one
- pixel_count: int32 [384], P(('pixel', 'crop')), may hold values from 16 to 32
- cloud_free: int32 [384, 52], P(('pixel', 'crop')), may hold values 0 or 1
- params: float32 [64, 8, 24], P('member'), may hold values from -6 to 6
- input_weight: bfloat16 [8, 48, 32], P('crop'), may hold values from -1 to 1
- conv_weight: bfloat16 [8, 3, 48, 96], P('crop'), may hold values from -0.625 to 0.625
- mix_weight: bfloat16 [8, 3, 48, 48], P('crop'), may hold values from -0.875 to 0.875
- head_weight: bfloat16 [8, 48], P('crop'), may hold values from -0.875 to 0.875
Outputs:
- updated: float32 [64, 8, 24], P('member', 'crop')
The draws below stay inside these ranges and needn't reach their ends.
Inputs may be any that keep to these rules, and one draw needn't show every extreme that they name: pixel_class is crop * 8 + region; among the 384 pixel places of one pixel and crop index no class is named more than 8 times, a bound that some block reaches. `cloud_free`: 1 where the block is seen in that week.
All inputs are finite; a program needn't handle non-finite values.
Results may differ from the reference program's by a relative error of at most 0.0067.
Values may be sent and summed in bfloat16 or wider, within the bound.
A program may use at most 128 MiB of HBM per device.

```python
import math
from functools import partial
import jax
import jax.numpy as jnp
import numpy as np
from jax import lax

WEEKS = 52
CHANNELS = 48
FORCING = 8
PARAMS = 24
LAYERS = 3
CROPS = 8
REGIONS = 8
BLK_PIX = 32
BLK_DEV = 12
MEMBERS = 64
CAP = 8
BLOCKS = 384
PIXELS = 12288
N_PIXEL = 4
N_CROP = 8


def plant(drawn, key, low, largest):
    shape = drawn.shape
    spot = [jax.random.randint(jax.random.fold_in(key, axis), (), 0, shape[axis]) for axis in range(len(shape))]
    drawn = drawn.at[tuple(spot)].set(low)
    longest = shape.index(max(shape))
    spot[longest] = (spot[longest] + 1) % shape[longest]
    return drawn.at[tuple(spot)].set(largest)


def shard_levels(rng, shape, pieces, smallest, high):
    factor_of = 1.0
    for axis_at, parts in pieces:
        heights = jax.random.uniform(jax.random.fold_in(jax.random.fold_in(rng, 6), axis_at), (parts,), jnp.float32, smallest / len(pieces), high / len(pieces))
        factor_of = factor_of * jnp.repeat(jnp.exp(heights), shape[axis_at] // parts).reshape((-1,) + (1,) * (len(shape) - 1 - axis_at))
    return factor_of


def routed_block(own_key, own, number, rows, count, top, reach, lean):
    sequence = jax.random.permutation(own_key, count)
    packed, common = portions_of(count, rows * top, reach, lean, True), portions_of(count, rows * top, reach, lean, False)
    places = jnp.arange(count)

    def named(lengths, offset_by):
        used = int((lengths > 0).sum())
        fixed = max(1, used // 4)
        passed = fixed + (places - fixed + offset_by * (used - fixed)) % max(1, count - fixed)
        return jnp.zeros((count,), jnp.int32).at[sequence[jnp.where(places < fixed, places, passed)]].set(jnp.asarray(lengths, jnp.int32))

    lengths = jnp.where(number % 4 == 0, named(packed, number // 4), named(common, number - number // 4 - 1))
    mixed = jax.random.permutation(jax.random.fold_in(own, 3), count)
    giver, taker = mixed[0:count // 2 * 2:2], mixed[1:count // 2 * 2:2]
    room = jnp.minimum(lengths[giver] - 1, reach - lengths[taker]) // 2
    room = jnp.where((giver == sequence[0]) | (taker == sequence[0]) | (lengths[taker] == 0), 0, jnp.maximum(room, 0))
    passed = jax.random.randint(jax.random.fold_in(own, 4), (count // 2,), 0, 1 << 20) % (room + 1)
    lengths = lengths.at[giver].add(-passed).at[taker].add(passed)
    items = jnp.searchsorted(jnp.cumsum(lengths), jnp.arange(rows * top), side="right").astype(jnp.int32)
    table = items.reshape(top, rows).T
    table = table[jax.random.permutation(jax.random.fold_in(own, 1), rows)]
    offset_by = jax.random.randint(jax.random.fold_in(own, 2), (rows, 1), 0, top)
    return jnp.take_along_axis(table, (jnp.arange(top)[None, :] + offset_by) % top, axis=1)


def portions_of(number_of, total, most, lean, full):
    portions = [(1 << 20) // math.isqrt(standing ** lean) + 1 for standing in range(1, number_of + 1)]
    largest = most if full else min(most, max(-(-total // number_of), total * portions[0] // sum(portions)))
    least = 1 if total - largest >= number_of - 1 else 0
    given, surplus = [largest] + [least] * (number_of - 1), total - largest - least * (number_of - 1)
    while surplus > 0:
        free = [i for i in range(1, number_of) if given[i] < largest] or [i for i in range(1, number_of) if given[i] < most]
        mass, left = sum([portions[i] for i in free]), surplus
        for i in free:
            more = min(most - given[i], max(1, left * portions[i] // mass), surplus)
            given[i] = given[i] + more
            surplus = surplus - more
    return np.array(given)


def bell_draw(key, shape, deviation, bound, split=(), kind=jnp.bfloat16):
    result = deviation * jax.random.normal(key, shape, jnp.float32)
    if split:
        result = result * shard_levels(key, shape, split, -0.22, 0.18)
    return jnp.clip(result, -bound, bound).astype(kind)


def setup_inputs(seed: int = 0) -> dict:
    key_of = jax.random.split(jax.random.key(seed), 12)
    forcing = bell_draw(key_of[0], (WEEKS, FORCING, PIXELS), 1.0, 6.0, ((2, 32),))
    observed = bell_draw(key_of[1], (WEEKS, PIXELS), 1.0, 6.0, ((1, 32),))
    obs_sigma = jnp.clip(jnp.exp(math.log(2.0) - 1.3862944 * jax.random.uniform(key_of[2], (PIXELS,), jnp.float32) ** shard_levels(key_of[2], (PIXELS,), ((0, 32),), -0.2, 0.2)), 0.5, 2.0)
    pixel_class_keys = jax.random.split(jax.random.fold_in(key_of[3], 1), PIXELS // (BLK_DEV * BLK_PIX))
    pixel_class_turns = jax.random.permutation(jax.random.fold_in(key_of[3], 3), PIXELS // (BLK_DEV * BLK_PIX))
    pixel_class = jax.vmap(lambda own, number: routed_block(jax.random.fold_in(key_of[3], 2), own, number, BLK_DEV * BLK_PIX, CROPS * REGIONS, 1, CAP, 2))(pixel_class_keys, pixel_class_turns).reshape((PIXELS, 1))
    pixel_count = plant(jax.random.randint(key_of[4], (BLOCKS,), BLK_PIX // 2, BLK_PIX + 1), jax.random.fold_in(key_of[4], 1), BLK_PIX // 2, BLK_PIX).astype(jnp.int32)
    cloud_free = plant((jax.random.randint(key_of[5], (BLOCKS, WEEKS), 0, 4) < 3).astype(jnp.int32), jax.random.fold_in(key_of[5], 1), 0, 1)
    params = bell_draw(key_of[6], (MEMBERS, REGIONS, PARAMS), 1.0, 6.0, ((0, 16),), jnp.float32)
    input_weight = bell_draw(key_of[7], (CROPS, CHANNELS, FORCING + PARAMS), (FORCING + PARAMS) ** -0.5, 1.0, ((0, 8),))
    conv_weight = bell_draw(key_of[8], (CROPS, LAYERS, CHANNELS, 2 * CHANNELS), (2 * CHANNELS) ** -0.5, 0.625, ((0, 8),))
    mix_weight = bell_draw(key_of[9], (CROPS, LAYERS, CHANNELS, CHANNELS), CHANNELS ** -0.5, 0.875, ((0, 8),))
    head_weight = bell_draw(key_of[10], (CROPS, CHANNELS), CHANNELS ** -0.5, 0.875, ((0, 8),))
    return dict(forcing=forcing, observed=observed, obs_sigma=obs_sigma, pixel_class=pixel_class, pixel_count=pixel_count, cloud_free=cloud_free, params=params, input_weight=input_weight, conv_weight=conv_weight, mix_weight=mix_weight, head_weight=head_weight)


ALPHA_INFLATION = 4.0

def pack_slots(forcing, observed, obs_sigma, pixel_class, pixel_count, cloud_free, n_class, cap_slots):
    n_blocks = pixel_count.shape[0]
    n_pixels = obs_sigma.shape[0]
    block_len = n_pixels // n_blocks
    classes = pixel_class[:, 0]
    position = jnp.arange(n_pixels, dtype=jnp.int32)
    is_live = position % block_len < jnp.repeat(pixel_count, block_len, total_repeat_length=n_pixels)
    earlier = (classes[None, :] == classes[:, None]) & is_live[None, :] & (position[None, :] < position[:, None])
    rank_in = lax.optimization_barrier(jnp.sum(earlier.astype(jnp.int32), axis=1))
    slot_of = classes * cap_slots + rank_in
    places = jnp.arange(n_class * cap_slots, dtype=jnp.int32)
    select = ((slot_of[:, None] == places[None, :]) & is_live[:, None]).astype(jnp.bfloat16)
    seen_mask = jnp.repeat(cloud_free, block_len, axis=0, total_repeat_length=n_pixels).astype(jnp.float32)
    obs_weight = (jnp.transpose(seen_mask) / obs_sigma[None, :]).astype(jnp.bfloat16)
    obs_pair = jnp.stack([observed, obs_weight], axis=1)
    sent_forcing = jnp.einsum('tfx,xs->tfs', forcing.astype(jnp.float32), select.astype(jnp.float32), preferred_element_type=jnp.float32).astype(jnp.bfloat16)
    sent_pair = jnp.einsum('tfx,xs->tfs', obs_pair.astype(jnp.float32), select.astype(jnp.float32), preferred_element_type=jnp.float32).astype(jnp.bfloat16)
    return (sent_forcing, sent_pair)

def run_network(slot_forcing, theta_member, region_hot, input_weight, conv_weight, mix_weight, head_weight):
    n_weeks = slot_forcing.shape[0]
    n_forcing = slot_forcing.shape[1]
    n_channels = conv_weight.shape[2]
    theta_bf = theta_member.astype(jnp.bfloat16)
    param_term = jnp.einsum('kcp,rp->ckr', input_weight[:, :, n_forcing:].astype(jnp.float32), theta_bf.astype(jnp.float32), preferred_element_type=jnp.float32)
    param_slot = lax.optimization_barrier(jnp.sum(param_term[:, :, :, None] * region_hot[None, None, :, :], axis=2))
    hidden = jnp.einsum('kcf,tfkq->tckq', input_weight[:, :, :n_forcing].astype(jnp.float32), slot_forcing.astype(jnp.float32), preferred_element_type=jnp.float32)
    hidden = (hidden + param_slot[None]).astype(jnp.bfloat16)
    for layer in range(conv_weight.shape[1]):
        dilation = 2 ** layer
        delayed = jnp.concatenate([jnp.zeros((dilation,) + hidden.shape[1:], jnp.bfloat16), hidden[:n_weeks - dilation]], axis=0)
        inner = jnp.einsum('koc,tckq->tokq', conv_weight[:, layer, :, :n_channels].astype(jnp.float32), hidden.astype(jnp.float32), preferred_element_type=jnp.float32)
        inner = inner + jnp.einsum('koc,tckq->tokq', conv_weight[:, layer, :, n_channels:].astype(jnp.float32), delayed.astype(jnp.float32), preferred_element_type=jnp.float32)
        inner = jax.nn.relu(inner).astype(jnp.bfloat16)
        mixed = jnp.einsum('koc,tckq->tokq', mix_weight[:, layer].astype(jnp.float32), inner.astype(jnp.float32), preferred_element_type=jnp.float32)
        hidden = (hidden.astype(jnp.float32) + mixed).astype(jnp.bfloat16)
    return jnp.einsum('kc,tckq->tkq', head_weight.astype(jnp.float32), hidden.astype(jnp.float32), preferred_element_type=jnp.float32)

def reference(forcing, observed, obs_sigma, pixel_class, pixel_count, cloud_free, params, input_weight, conv_weight, mix_weight, head_weight):
    sources = N_PIXEL * N_CROP
    n_weeks, n_forcing, n_pixels = forcing.shape
    per_source = n_pixels // sources
    per_class = REGIONS * CAP
    packer = partial(pack_slots, n_class=CROPS * REGIONS, cap_slots=CAP)
    packed_forcing, packed_pair = jax.vmap(packer, in_axes=(2, 1, 0, 0, 0, 0))(forcing.reshape(n_weeks, n_forcing, sources, per_source), observed.reshape(n_weeks, sources, per_source), obs_sigma.reshape(sources, per_source), pixel_class.reshape(sources, per_source, 1), pixel_count.reshape(sources, -1), cloud_free.reshape(sources, -1, n_weeks))
    slot_forcing = jnp.transpose(packed_forcing.reshape(sources, n_weeks, n_forcing, CROPS, per_class), (1, 2, 3, 0, 4))
    slot_forcing = slot_forcing.reshape(n_weeks, n_forcing, CROPS, sources * per_class)
    slot_pair = jnp.transpose(packed_pair.reshape(sources, n_weeks, 2, CROPS, per_class), (1, 2, 3, 0, 4))
    slot_pair = slot_pair.reshape(n_weeks, 2, -1)
    width_q = sources * per_class
    region_ids = jnp.arange(REGIONS, dtype=jnp.int32)
    region_hot = (jnp.arange(width_q, dtype=jnp.int32) // CAP % REGIONS == region_ids[:, None]).astype(jnp.float32)

    def run_member(theta_member):
        return run_network(slot_forcing, theta_member, region_hot, input_weight, conv_weight, mix_weight, head_weight)
    members = params.shape[0]
    predicted = lax.map(run_member, params).reshape(members, n_weeks, -1)
    n_slots = predicted.shape[2]
    mean_pred = lax.optimization_barrier(jnp.sum(predicted, axis=0)) / members
    obs_value = slot_pair[:, 0].astype(jnp.float32)
    obs_weight = slot_pair[:, 1].astype(jnp.float32)
    scaled = (obs_weight[None] * (predicted - mean_pred[None]) / math.sqrt(ALPHA_INFLATION * (members - 1))).astype(jnp.bfloat16)
    innovation = obs_weight * (obs_value - mean_pred) / math.sqrt(ALPHA_INFLATION)
    slot_region = jnp.arange(n_slots, dtype=jnp.int32) // CAP % REGIONS
    flat_rows = scaled.reshape(members, -1)
    flat_wide = flat_rows.astype(jnp.float32)
    flat_innov = innovation.reshape(-1)

    def region_terms(region):
        in_region = jnp.broadcast_to(slot_region[None, :] == region, (n_weeks, n_slots)).reshape(-1)
        masked = jnp.where(in_region[None, :], flat_rows, jnp.zeros((), jnp.bfloat16))
        gram_block = jnp.dot(masked.astype(jnp.float32), jnp.transpose(flat_rows).astype(jnp.float32), preferred_element_type=jnp.float32)
        proj_block = jnp.dot(flat_wide, jnp.where(in_region, flat_innov, jnp.zeros((), flat_innov.dtype)), precision=lax.Precision.HIGHEST)
        return (gram_block, proj_block)
    grams, projs = lax.map(region_terms, region_ids)
    scale_root = math.sqrt(members - 1)

    def update(gram_block, proj_block, theta_region):
        system = gram_block + jnp.eye(members, dtype=gram_block.dtype)
        factor = jnp.linalg.cholesky(system)
        right_side = proj_block[:, None] - scale_root * gram_block
        mixing = jax.scipy.linalg.cho_solve((factor, True), right_side)
        spread = (theta_region - lax.optimization_barrier(jnp.sum(theta_region, axis=0)) / members) / scale_root
        return theta_region + jnp.dot(jnp.transpose(mixing), spread, precision=lax.Precision.HIGHEST)
    return jax.vmap(update, in_axes=(0, 0, 1), out_axes=1)(grams, projs, params)
```

```python
import functools
import math

import jax
import jax.numpy as jnp
from jax import lax
from jax.experimental import pallas as pl
from jax.experimental.pallas import tpu as pltpu
from jax.sharding import PartitionSpec as P

MESH = pl.DeviceIdType.MESH
F32 = jnp.float32
BF16 = jnp.bfloat16
WEEKS = 52
CH = 48
NF = 8
NP = 24
CAP = 8
BLK = 32
ALPHA_INFLATION = 4.0
HALF = CAP // 2
SLOTS = 32
MSUB = 4
LANES = MSUB * SLOTS
ROW = 640
OBS_AT = 512
WGT_AT = 576
PAD = 4


def iota(shape, dim):
    return lax.broadcasted_iota(jnp.int32, shape, dim)


def nt(a, b):
    return lax.dot_general(a, b, (((1,), (1,)), ((), ())), preferred_element_type=F32)


def tn(a, b):
    return lax.dot_general(a, b, (((0,), (0,)), ((), ())), preferred_element_type=F32)


def hi_lo(x):
    hi = x.astype(BF16)
    return hi, (x - hi.astype(F32)).astype(BF16)


def pack_kernel(
    n_crop, n_member,
    forcing, observed, sigma, classes, counts, cloud, params,
    got, pars,
    rows, message, par_message, send, recv, par_send, par_recv,
):
    crop = lax.axis_index("crop")
    member = lax.axis_index("member")
    region = member // 2
    half = member % 2
    pixels = rows.shape[1]
    blocks = cloud.shape[0]

    barrier = pltpu.get_barrier_semaphore()
    for k in range(1, n_crop):
        pl.semaphore_signal(
            barrier, inc=1, device_id={"crop": (crop + k) % n_crop}, device_id_type=MESH
        )
    for k in range(1, n_member):
        pl.semaphore_signal(
            barrier, inc=1, device_id={"member": (member + k) % n_member}, device_id_type=MESH
        )

    own = params[...]
    par_message[...] = jnp.zeros_like(par_message)
    for j in range(n_member):
        par_message[j, :, :NP] = own[:, j // 2, :]
        par_message[j, :, 128 : 128 + NP] = params[:, crop, :]
    pl.semaphore_wait(barrier, n_crop - 1 + n_member - 1)
    par_copies = []
    for k in range(1, n_member):
        target = (member + k) % n_member
        copy = pltpu.make_async_remote_copy(
            src_ref=par_message.at[target],
            dst_ref=pars.at[member],
            send_sem=par_send.at[k],
            recv_sem=par_recv.at[member],
            device_id={"member": target},
            device_id_type=MESH,
        )
        copy.start()
        par_copies.append(copy)

    place = iota((1, pixels), 1)
    limit = jnp.zeros((1, pixels), jnp.int32)
    for b in range(blocks):
        limit = jnp.where(place // BLK == b, counts[b], limit)
    live = place % BLK < limit
    slots = n_crop * HALF
    slot = iota((slots, pixels), 0)
    named = (classes[...] == (slot // HALF) * 8 + region) & live
    named = jnp.where(named, 1.0, 0.0)
    before = jnp.where(iota((pixels, pixels), 0) < iota((pixels, pixels), 1), 1.0, 0.0)
    rank = jnp.dot(named.astype(BF16), before.astype(BF16), preferred_element_type=F32)
    wanted = (slot % HALF + half * HALF).astype(F32)
    select = jnp.where(rank == wanted, named, 0.0).astype(BF16)

    in_block = iota((blocks, pixels), 1) // BLK == iota((blocks, pixels), 0)
    seen = tn(cloud[...].astype(F32).astype(BF16), jnp.where(in_block, 1.0, 0.0).astype(BF16))
    rows[...] = jnp.zeros_like(rows)
    rows[: WEEKS * NF, :] = forcing[...].astype(F32).reshape(WEEKS * NF, pixels)
    rows[OBS_AT : OBS_AT + WEEKS, :] = observed[...].astype(F32)
    rows[WGT_AT : WGT_AT + WEEKS, :] = seen / sigma[...]
    packed = nt(select, rows[...].astype(BF16))
    for c in range(n_crop):
        message[c] = packed[HALF * c : HALF * (c + 1), :]

    copies = []
    for k in range(1, n_crop):
        target = (crop + k) % n_crop
        copy = pltpu.make_async_remote_copy(
            src_ref=message.at[target],
            dst_ref=got.at[k],
            send_sem=send.at[k],
            recv_sem=recv.at[k],
            device_id={"crop": target},
            device_id_type=MESH,
        )
        copy.start()
        copies.append(copy)
    got[0] = message[crop]
    pars[member] = par_message[member]

    for k in range(1, n_member):
        source = (member + k) % n_member
        pltpu.make_async_remote_copy(
            src_ref=par_message.at[source],
            dst_ref=pars.at[source],
            send_sem=par_send.at[k],
            recv_sem=par_recv.at[source],
            device_id={"member": source},
            device_id_type=MESH,
        ).wait_recv()
    for copy in par_copies:
        copy.wait_send()
    for copy in copies:
        copy.wait()


def network_kernel(
    got, pars, input_weight, conv_weight, mix_weight, head_weight,
    gram,
    stacked, ft, fpart, gpart, ghead, thetas, inner0, inner1, pred, ext,
):
    members = gram.shape[0]
    groups = members // MSUB
    width = groups * LANES
    tiles = width // 256

    mixes = [mix_weight[0, l] for l in range(3)]
    convs = [conv_weight[0, l] for l in range(3)]
    cur = [c[:, :CH] for c in convs]
    old = [c[:, CH:] for c in convs]
    head = head_weight[...]

    def dot(a, b):
        return jnp.dot(a, b, preferred_element_type=F32)

    w_in16 = input_weight[0]
    cur_in = [dot(a, w_in16) for a in cur]
    old_in = [dot(a, w_in16) for a in old]
    head_in = dot(head, w_in16)
    w1 = jnp.concatenate([dot(cur[1], mixes[0]), dot(old[1], mixes[0])], axis=1)
    w2 = jnp.concatenate(
        [
            dot(cur[2], mixes[0]),
            dot(old[2], mixes[0]),
            dot(cur[2], mixes[1]),
            dot(old[2], mixes[1]),
        ],
        axis=1,
    )
    head_mix = [dot(head, m) for m in mixes]
    zero_row = jnp.zeros((1, CH), F32)
    head2 = jnp.concatenate([head_mix[0], zero_row, head_mix[1], zero_row], axis=1)
    w1_hi, w1_lo = hi_lo(w1)
    w1_all = jnp.concatenate([w1_hi, w1_lo], axis=0)
    w2_hi, w2_lo = hi_lo(w2)
    h2_hi, h2_lo = hi_lo(jnp.broadcast_to(head2, (16, 4 * CH)))
    h2_all = jnp.where(
        iota((16, 4 * CH), 0) == 0,
        h2_hi.astype(F32),
        jnp.where(iota((16, 4 * CH), 0) == 1, h2_lo.astype(F32), 0.0),
    ).astype(BF16)
    w2_all = jnp.concatenate([w2_hi, w2_lo, h2_all], axis=0)

    for a in range(MSUB):
        for k in range(SLOTS // HALF):
            at = a * SLOTS + k * HALF
            stacked[at : at + HALF, :] = got[k]
    ft[: PAD * NF, :] = jnp.zeros((PAD * NF, LANES), F32)
    ft[PAD * NF :, :] = jnp.transpose(stacked[...])

    lf = []
    for l in range(3):
        part = jnp.concatenate([cur_in[l][:, :NF], old_in[l][:, :NF]], axis=1)
        if l == 0:
            top = jnp.concatenate([head_in[:, :NF], jnp.zeros((1, NF), F32)], axis=1)
            part = jnp.concatenate([part, jnp.broadcast_to(top, (8, 2 * NF))], axis=0)
        hi = part.astype(BF16).astype(F32)
        lf.append(jnp.concatenate([hi, part - hi], axis=1).astype(BF16))

    def forcing_part(t, carry):
        now = ft[pl.ds((t + PAD) * NF, NF), :]
        for l in range(3):
            late = ft[pl.ds((t + PAD - 2**l) * NF, NF), :]
            x = jnp.concatenate([now, late, now, late], axis=0).astype(BF16)
            y = dot(lf[l], x)
            if l == 0:
                fpart[t, 3 * CH : 3 * CH + 8, :] = y[CH:, :]
            fpart[t, l * CH : (l + 1) * CH, :] = y[:CH, :]
        return carry

    lax.fori_loop(0, WEEKS, forcing_part, 0)

    for g in range(groups):
        thetas[g * MSUB : (g + 1) * MSUB, :] = pars[g, :, :128]
    theta = thetas[...][:, :32].astype(BF16)
    spread = jnp.where(iota((members, width), 1) // SLOTS == iota((members, width), 0), 1.0, 0.0)
    theta_wide = tn(theta, spread.astype(BF16))
    theta_twice = jnp.concatenate([theta_wide, theta_wide], axis=0).astype(BF16)

    def theta_weight(x):
        x = jnp.concatenate([x[:, NF:], jnp.zeros((x.shape[0], 8), F32)], axis=1)
        hi = x.astype(BF16).astype(F32)
        return jnp.concatenate([hi, x - hi], axis=1).astype(BF16)

    for l in range(3):
        gpart[2 * l] = dot(theta_weight(cur_in[l]), theta_twice)
        gpart[2 * l + 1] = dot(theta_weight(cur_in[l] + old_in[l]), theta_twice)
    ghead[...] = dot(theta_weight(jnp.broadcast_to(head_in, (8, 32))), theta_twice)

    inner0[:PAD] = jnp.zeros((PAD, CH, width), BF16)
    inner1[:PAD] = jnp.zeros((PAD, CH, width), BF16)
    last = jnp.transpose(jnp.broadcast_to(head_mix[2], (128, CH)))
    last = jnp.concatenate([last, last], axis=1)

    def twice(x):
        return jnp.concatenate([x, x], axis=1)

    def layer01(t, carry):
        g0 = jnp.where(t >= 1, 1, 0)
        g1 = jnp.where(t >= 2, 3, 2)
        f = fpart[t]
        for j in range(tiles):
            at = pl.ds(j * 256, 256)
            x0 = jnp.maximum(twice(f[:CH]) + gpart[g0, :, at], 0.0).astype(BF16)
            inner0[t + PAD, :, at] = x0
            x = jnp.concatenate([x0, inner0[t + PAD - 2, :, at]], axis=0)
            y = dot(w1_all, x)
            y = y[:CH] + y[CH:] + (twice(f[CH : 2 * CH]) + gpart[g1, :, at])
            inner1[t + PAD, :, at] = jnp.maximum(y, 0.0).astype(BF16)
        return carry

    lax.fori_loop(0, WEEKS, layer01, 0)

    def layer2(t, carry):
        g2 = jnp.where(t >= 4, 5, 4)
        f = fpart[t]
        for j in range(tiles):
            at = pl.ds(j * 256, 256)
            x = jnp.concatenate(
                [
                    inner0[t + PAD, :, at],
                    inner0[t + PAD - 4, :, at],
                    inner1[t + PAD, :, at],
                    inner1[t + PAD - 4, :, at],
                ],
                axis=0,
            )
            y = dot(w2_all, x)
            z = y[:CH] + y[CH : 2 * CH] + (twice(f[2 * CH : 3 * CH]) + gpart[g2, :, at])
            z = jnp.maximum(z, 0.0) * last
            out = jnp.sum(z, axis=0, keepdims=True)
            out = out + y[2 * CH : 2 * CH + 1] + y[2 * CH + 1 : 2 * CH + 2]
            out = out + twice(f[3 * CH : 3 * CH + 1]) + ghead[:1, at]
            pred[t, 2 * j : 2 * j + 1, :] = out[:, :LANES]
            pred[t, 2 * j + 1 : 2 * j + 2, :] = out[:, LANES:]
        return carry

    lax.fori_loop(0, WEEKS, layer2, 0)

    p = pred[...]
    total = jnp.sum(p, axis=1)
    total = total + pltpu.roll(total, 2 * SLOTS, 1)
    total = total + pltpu.roll(total, SLOTS, 1)
    mean = total / members
    base = PAD * NF
    obs = ft[base + OBS_AT : base + OBS_AT + WEEKS, :]
    wgt = ft[base + WGT_AT : base + WGT_AT + WEEKS, :]
    innovation = wgt * (obs - mean) / math.sqrt(ALPHA_INFLATION)
    factor = wgt / math.sqrt(ALPHA_INFLATION * (members - 1))
    pred[...] = (p - mean[:, None, :]) * factor[:, None, :]

    block = iota((groups, LANES), 1) // SLOTS
    ext[members:, :] = jnp.zeros((ext.shape[0] - members, ext.shape[1]), BF16)
    block8 = iota((8, LANES), 1) // SLOTS
    row8 = iota((8, LANES), 0)
    for q in range(WEEKS // MSUB):
        weeks = [pred[MSUB * q + b] for b in range(MSUB)]
        parts = []
        for a in range(MSUB):
            out = weeks[a]
            for b in range(MSUB):
                if b != a:
                    moved = pltpu.roll(weeks[b], (b - a) % MSUB * SLOTS, 1)
                    out = jnp.where(block == b, moved, out)
            parts.append(out)
        cols = slice(LANES * q, LANES * (q + 1))
        ext[:members, cols] = jnp.concatenate(parts, axis=0).astype(BF16)
        inn = jnp.zeros((8, LANES), F32)
        for b in range(MSUB):
            line = jnp.broadcast_to(innovation[MSUB * q + b : MSUB * q + b + 1], (8, LANES))
            inn = jnp.where(block8 == b, line, inn)
        hi = inn.astype(BF16).astype(F32)
        inn = jnp.where(row8 == 0, hi, jnp.where(row8 == 1, inn - hi, 0.0))
        inn = jnp.concatenate([inn, jnp.zeros((8, LANES), F32)], axis=0)
        ext[members : members + 16, cols] = inn.astype(BF16)
    gram[...] = nt(ext[:members, :], ext[...])


def reduce_kernel(
    n_pixel, n_crop, n_member,
    gram, pars, out,
    part, one, every, final, spread_rows, solved,
    send_a, recv_a, send_b, recv_b, send_c, recv_c,
):
    pixel = lax.axis_index("pixel")
    crop = lax.axis_index("crop")
    member = lax.axis_index("member")
    region = member // 2
    half = member % 2
    mine = pixel * 2 + half
    peers = 2 * n_pixel
    members = spread_rows.shape[0]
    groups = members // MSUB

    def peer(k):
        q = (mine + k) % peers
        return q, {"pixel": q // 2, "member": region * 2 + q % 2}

    barrier = pltpu.get_barrier_semaphore()
    for k in range(1, n_crop):
        pl.semaphore_signal(
            barrier, inc=1, device_id={"crop": (crop + k) % n_crop}, device_id_type=MESH
        )
    for k in range(1, peers):
        pl.semaphore_signal(barrier, inc=1, device_id=peer(k)[1], device_id_type=MESH)
    for k in range(1, n_crop):
        source = (crop + k) % n_crop
        pl.semaphore_signal(
            barrier, inc=1,
            device_id={"crop": source, "member": crop * 2 + half}, device_id_type=MESH,
        )

    @pl.when(region != crop)
    def _():
        pl.semaphore_signal(
            barrier, inc=1, device_id={"member": crop * 2 + half}, device_id_type=MESH
        )

    pl.semaphore_wait(
        barrier, n_crop - 1 + peers - 1 + n_crop - 1 + jnp.where(region != crop, 1, 0)
    )

    copies = []
    for k in range(1, n_crop):
        target = (crop + k) % n_crop
        copy = pltpu.make_async_remote_copy(
            src_ref=gram.at[target],
            dst_ref=part.at[k],
            send_sem=send_a.at[k],
            recv_sem=recv_a.at[k],
            device_id={"crop": target},
            device_id_type=MESH,
        )
        copy.start()
        copies.append(copy)

    for g in range(groups):
        block = pars[g]
        for a in range(MSUB):
            spread_rows[a * groups + g : a * groups + g + 1, :] = block[a : a + 1, 128:]
    theta = spread_rows[...]
    mean = jnp.sum(theta, axis=0, keepdims=True) / members
    spread = (theta - mean) / math.sqrt(members - 1)

    acc = gram[crop]
    for copy in copies:
        copy.wait()
    for k in range(1, n_crop):
        acc = acc + part[k]
    one[...] = acc
    copies = []
    for k in range(1, peers):
        q, where = peer(k)
        copy = pltpu.make_async_remote_copy(
            src_ref=one,
            dst_ref=every.at[mine],
            send_sem=send_b.at[k],
            recv_sem=recv_b.at[mine],
            device_id=where,
            device_id_type=MESH,
        )
        copy.start()
        copies.append(copy)
    every[mine] = acc
    for copy in copies:
        copy.wait_send()
    for k in range(1, peers):
        q, where = peer(k)
        pltpu.make_async_remote_copy(
            src_ref=one,
            dst_ref=every.at[q],
            send_sem=send_b.at[k],
            recv_sem=recv_b.at[q],
            device_id=where,
            device_id_type=MESH,
        ).wait_recv()
    acc = every[0]
    for q in range(1, peers):
        acc = acc + every[q]
    one[...] = acc

    def row_copy(j):
        return pltpu.make_async_remote_copy(
            src_ref=one,
            dst_ref=final.at[crop],
            send_sem=send_c.at[j],
            recv_sem=recv_c.at[crop],
            device_id={"crop": region, "member": j * 2 + half},
            device_id_type=MESH,
        )

    regions = n_member // 2
    for k in range(1, regions):
        row_copy((region + k) % regions).start()

    @pl.when(region != crop)
    def _():
        row_copy(region).start()

    @pl.when(region == crop)
    def _():
        final[crop] = one[...]

    for k in range(1, regions):
        row_copy((region + k) % regions).wait_send()

    @pl.when(region != crop)
    def _():
        row_copy(region).wait_send()

    def row_arrival(source):
        return pltpu.make_async_remote_copy(
            src_ref=one,
            dst_ref=final.at[source],
            send_sem=send_c.at[source],
            recv_sem=recv_c.at[source],
            device_id={"crop": source, "member": crop * 2 + half},
            device_id_type=MESH,
        )

    for k in range(1, n_crop):
        row_arrival((crop + k) % n_crop).wait_recv()

    @pl.when(region != crop)
    def _():
        row_arrival(crop).wait_recv()

    whole = final[...].reshape(members, 128)
    proj = whole[:, members : members + 1] + whole[:, members + 1 : members + 2]
    lane = iota((members, 128), 1)
    row = iota((members, 128), 0)
    moved = pltpu.roll(spread, members, 1)
    system = jnp.where(lane < members, whole + jnp.where(lane == row, 1.0, 0.0), moved)
    for k in range(members):
        line = system[k : k + 1, :]
        line = line / line[:, k : k + 1]
        column = system[:, k : k + 1]
        factor = jnp.broadcast_to(column, (members, 128)) - jnp.where(row == k, 1.0, 0.0)
        system = system - factor * line
    y = jnp.where(lane >= members, system, 0.0)
    y = pltpu.roll(y, 128 - members, 1)
    solved[...] = y
    shared = mean + jnp.sum(proj * y, axis=0, keepdims=True)
    for a in range(MSUB):
        own = solved[pl.ds(a * groups + member, 1), :]
        result = shared + math.sqrt(members - 1) * own
        out[a] = result[:, :NP]


def local(
    sizes,
    forcing, observed, obs_sigma, pixel_class, pixel_count, cloud_free, params,
    input_weight, conv_weight, mix_weight, head_weight,
):
    n_pixel, n_crop, n_member = sizes
    pixels = obs_sigma.shape[0]
    members = params.shape[0] * n_member
    groups = members // MSUB
    width = groups * LANES
    vmem = pl.BlockSpec(memory_space=pltpu.VMEM)
    smem = pl.BlockSpec(memory_space=pltpu.SMEM)
    got, pars = pl.pallas_call(
        functools.partial(pack_kernel, n_crop, n_member),
        name="pack",
        out_shape=(
            jax.ShapeDtypeStruct((n_crop, HALF, ROW), F32),
            jax.ShapeDtypeStruct((n_member, MSUB, 256), F32),
        ),
        in_specs=[vmem, vmem, vmem, vmem, smem, vmem, vmem],
        out_specs=(vmem, vmem),
        scratch_shapes=[
            pltpu.VMEM((ROW, pixels), F32),
            pltpu.VMEM((n_crop, HALF, ROW), F32),
            pltpu.VMEM((n_member, MSUB, 256), F32),
            pltpu.SemaphoreType.DMA((n_crop,)),
            pltpu.SemaphoreType.DMA((n_crop,)),
            pltpu.SemaphoreType.DMA((n_member,)),
            pltpu.SemaphoreType.DMA((n_member,)),
        ],
        compiler_params=pltpu.CompilerParams(collective_id=0, has_side_effects=True),
    )(
        forcing, observed, obs_sigma.reshape(1, pixels), pixel_class.reshape(1, pixels),
        pixel_count, cloud_free, params,
    )
    gram = pl.pallas_call(
        network_kernel,
        name="network",
        out_shape=jax.ShapeDtypeStruct((members, 128), F32),
        in_specs=[vmem] * 6,
        out_specs=vmem,
        scratch_shapes=[
            pltpu.VMEM((LANES, ROW), F32),
            pltpu.VMEM((PAD * NF + ROW, LANES), F32),
            pltpu.VMEM((WEEKS, 3 * CH + 8, LANES), F32),
            pltpu.VMEM((6, CH, width), F32),
            pltpu.VMEM((8, width), F32),
            pltpu.VMEM((members, 128), F32),
            pltpu.VMEM((PAD + WEEKS, CH, width), BF16),
            pltpu.VMEM((PAD + WEEKS, CH, width), BF16),
            pltpu.VMEM((WEEKS, groups, LANES), F32),
            pltpu.VMEM((128, WEEKS // MSUB * LANES), BF16),
        ],
        compiler_params=pltpu.CompilerParams(vmem_limit_bytes=52 << 20),
    )(got, pars, input_weight, conv_weight, mix_weight, head_weight)
    return pl.pallas_call(
        functools.partial(reduce_kernel, n_pixel, n_crop, n_member),
        name="reduce",
        out_shape=jax.ShapeDtypeStruct((MSUB, 1, NP), F32),
        in_specs=[vmem, vmem],
        out_specs=vmem,
        scratch_shapes=[
            pltpu.VMEM((n_crop, 8, 128), F32),
            pltpu.VMEM((8, 128), F32),
            pltpu.VMEM((2 * n_pixel, 8, 128), F32),
            pltpu.VMEM((n_crop, 8, 128), F32),
            pltpu.VMEM((members, 128), F32),
            pltpu.VMEM((members, 128), F32),
            pltpu.SemaphoreType.DMA((n_crop,)),
            pltpu.SemaphoreType.DMA((n_crop,)),
            pltpu.SemaphoreType.DMA((2 * n_pixel,)),
            pltpu.SemaphoreType.DMA((2 * n_pixel,)),
            pltpu.SemaphoreType.DMA((n_crop,)),
            pltpu.SemaphoreType.DMA((n_crop,)),
        ],
        compiler_params=pltpu.CompilerParams(collective_id=1, has_side_effects=True),
    )(gram.reshape(n_crop, 8, 128), pars)


def solution(mesh):
    sizes = (mesh.shape["pixel"], mesh.shape["crop"], mesh.shape["member"])
    in_specs = (
        P(None, None, ("pixel", "crop")),
        P(None, ("pixel", "crop")),
        P(("pixel", "crop")),
        P(("pixel", "crop"), None),
        P(("pixel", "crop")),
        P(("pixel", "crop"), None),
        P("member", None, None),
        P("crop", None, None),
        P("crop", None, None, None),
        P("crop", None, None, None),
        P("crop", None),
    )
    return jax.shard_map(
        functools.partial(local, sizes),
        mesh=mesh,
        in_specs=in_specs,
        out_specs=P("member", "crop", None),
        check_vma=False,
    )
```

```python
import functools
import math

import jax
import jax.numpy as jnp
from jax import lax
from jax.experimental import pallas as pl
from jax.experimental.pallas import tpu as pltpu
from jax.sharding import PartitionSpec as P

MESH = pl.DeviceIdType.MESH
F32 = jnp.float32
BF16 = jnp.bfloat16
WEEKS = 52
CH = 48
NF = 8
NP = 24
CAP = 8
BLK = 32
ALPHA_INFLATION = 4.0
HALF = CAP // 2
SLOTS = 32
MSUB = 4
LANES = MSUB * SLOTS
ROW = 640
OBS_AT = 512
WGT_AT = 576
PAD = 4


def iota(shape, dim):
    return lax.broadcasted_iota(jnp.int32, shape, dim)


def nt(a, b):
    return lax.dot_general(a, b, (((1,), (1,)), ((), ())), preferred_element_type=F32)


def tn(a, b):
    return lax.dot_general(a, b, (((0,), (0,)), ((), ())), preferred_element_type=F32)


def hi_lo(x):
    hi = x.astype(BF16)
    return hi, (x - hi.astype(F32)).astype(BF16)


def mega_kernel(
    n_pixel, n_crop,
    forcing_hbm, observed_hbm, sigma_hbm, classes_hbm, counts, cloud_hbm, params_hbm,
    input_hbm, conv_hbm, mix_hbm, head_hbm,
    out,
    forcing, observed, sigma, classes, cloud, params, input_weight, conv_weight, mix_weight,
    head_weight,
    rows, message, got, near, merged, far_message, pars, theta_rows,
    stacked, ft, fpart, gpart, ghead, inner0, inner1, pred, ext,
    gram, part, one, every, final, spread_rows, solved,
    load, send, recv, near_send, near_recv, far_send, far_recv,
    send_a, recv_a, send_b, recv_b, send_c, recv_c,
):
    pixel = lax.axis_index("pixel")
    crop = lax.axis_index("crop")
    member = lax.axis_index("member")
    x_at = member // 4
    z_high = member % 4
    z_low = crop // 2
    core = crop % 2
    region = z_high * 2 + x_at // 2
    half = x_at % 2
    pixels = rows.shape[1]
    blocks = cloud.shape[0]
    peers = 2 * n_pixel
    mine = pixel * 2 + half
    members = spread_rows.shape[0]
    groups = members // MSUB
    width = groups * LANES
    tiles = width // 256

    def dot(a, b):
        return jnp.dot(a, b, preferred_element_type=F32)

    def remote(src, dst, send_sem, recv_sem, where):
        return pltpu.make_async_remote_copy(
            src_ref=src, dst_ref=dst, send_sem=send_sem, recv_sem=recv_sem,
            device_id=where, device_id_type=MESH,
        )

    loads = []
    pairs = (
        (params_hbm, params), (forcing_hbm, forcing), (observed_hbm, observed),
        (sigma_hbm, sigma), (classes_hbm, classes), (cloud_hbm, cloud),
        (input_hbm, input_weight), (conv_hbm, conv_weight), (mix_hbm, mix_weight),
        (head_hbm, head_weight),
    )
    for i, (src, dst) in enumerate(pairs):
        copy = pltpu.make_async_copy(src, dst, load.at[i])
        copy.start()
        loads.append(copy)

    def crop_peer(k):
        return {"crop": (crop + k) % n_crop}

    def x_peer(k):
        return {"member": (x_at + k) % 4 * 4 + z_high}

    def sum_peer(k):
        q = (mine + k) % peers
        return q, {"pixel": q // 2, "member": (x_at // 2 * 2 + q % 2) * 4 + z_high}

    inside = (z_low == 1) | (z_low == 2)
    slab = jnp.where(z_low == 2, 1, jnp.where(z_low == 1, 3, 2))

    def far_target(k):
        z_to = k + jnp.where(z_low == 0, 2, 0)
        high = (z_high + slab) % 4
        return high * 2 + x_at // 2, z_to * 2 + core, {
            "crop": z_to * 2 + core, "member": x_at * 4 + high
        }

    def far_source(k):
        z_from = (1, jnp.where(z_low < 2, 3, 0), 2)[k - 1]
        high = (z_high + k) % 4
        return high, {"crop": z_from * 2 + core, "member": x_at * 4 + high}

    barrier = pltpu.get_barrier_semaphore()
    for k in range(1, 4):
        pl.semaphore_signal(barrier, inc=1, device_id=far_source(k)[1], device_id_type=MESH)
    for k in range(1, n_crop):
        pl.semaphore_signal(barrier, inc=1, device_id=crop_peer(k), device_id_type=MESH)
    for k in range(1, 4):
        pl.semaphore_signal(barrier, inc=1, device_id=x_peer(k), device_id_type=MESH)
    for k in range(1, peers):
        pl.semaphore_signal(barrier, inc=1, device_id=sum_peer(k)[1], device_id_type=MESH)

    loads[0].wait()
    quarter = iota((8, 128), 1) // 32
    for a in range(MSUB):
        block = jnp.concatenate([params[a], jnp.zeros((8, 32 - NP), F32)], axis=1)
        block = jnp.concatenate([block] * 4, axis=1)
        near[x_at, a] = jnp.where(quarter == x_at, block, 0.0)

    for copy in loads[1:6]:
        copy.wait()
    place = iota((1, pixels), 1)
    limit = jnp.zeros((1, pixels), jnp.int32)
    for b in range(blocks):
        limit = jnp.where(place // BLK == b, counts[b], limit)
    live = place % BLK < limit
    slots = n_crop * HALF
    slot = iota((slots, pixels), 0)
    named = (classes[...] == (slot // HALF) * 8 + region) & live
    named = jnp.where(named, 1.0, 0.0)
    before = jnp.where(iota((pixels, pixels), 0) < iota((pixels, pixels), 1), 1.0, 0.0)
    rank = dot(named.astype(BF16), before.astype(BF16))
    wanted = (slot % HALF + half * HALF).astype(F32)
    select = jnp.where(rank == wanted, named, 0.0).astype(BF16)

    in_block = iota((blocks, pixels), 1) // BLK == iota((blocks, pixels), 0)
    seen = tn(cloud[...].astype(F32).astype(BF16), jnp.where(in_block, 1.0, 0.0).astype(BF16))
    rows[...] = jnp.zeros_like(rows)
    rows[: WEEKS * NF, :] = forcing[...].astype(F32).reshape(WEEKS * NF, pixels)
    rows[OBS_AT : OBS_AT + WEEKS, :] = observed[...].astype(F32)
    rows[WGT_AT : WGT_AT + WEEKS, :] = seen / sigma[...].reshape(1, pixels)
    packed = nt(select, rows[...].astype(BF16))
    for c in range(n_crop):
        message[c] = packed[HALF * c : HALF * (c + 1), :]

    pl.semaphore_wait(barrier, 3 + n_crop - 1 + peers - 1 + jnp.where(inside, 4, 2))
    near_copies = [
        remote(near.at[x_at], near.at[x_at], near_send.at[k], near_recv.at[x_at], x_peer(k))
        for k in range(1, 4)
    ]
    for copy in near_copies:
        copy.start()
    copies = []
    for k in range(1, n_crop):
        where = crop_peer(k)
        copy = remote(message.at[where["crop"]], got.at[k], send.at[k], recv.at[k], where)
        copy.start()
        copies.append(copy)
    got[0] = message[crop]

    for copy in loads[6:]:
        copy.wait()
    mixes = [mix_weight[0, l] for l in range(3)]
    convs = [conv_weight[0, l] for l in range(3)]
    cur = [c[:, :CH] for c in convs]
    old = [c[:, CH:] for c in convs]
    head = head_weight[...]
    w_in = input_weight[0]
    cur_in = [nt(a, w_in) for a in cur]
    old_in = [nt(a, w_in) for a in old]
    head_in = nt(head, w_in)
    w1 = jnp.concatenate([dot(cur[1], mixes[0]), dot(old[1], mixes[0])], axis=1)
    w2 = jnp.concatenate(
        [
            dot(cur[2], mixes[0]),
            dot(old[2], mixes[0]),
            dot(cur[2], mixes[1]),
            dot(old[2], mixes[1]),
        ],
        axis=1,
    )
    head_mix = [dot(head, m) for m in mixes]
    zero_row = jnp.zeros((1, CH), F32)
    head2 = jnp.concatenate([head_mix[0], zero_row, head_mix[1], zero_row], axis=1)
    w1_hi, w1_lo = hi_lo(w1)
    w1_all = jnp.concatenate([w1_hi, w1_lo], axis=0)
    w2_hi, w2_lo = hi_lo(w2)
    h2_hi, h2_lo = hi_lo(jnp.broadcast_to(head2, (16, 4 * CH)))
    h2_all = jnp.where(
        iota((16, 4 * CH), 0) == 0,
        h2_hi.astype(F32),
        jnp.where(iota((16, 4 * CH), 0) == 1, h2_lo.astype(F32), 0.0),
    ).astype(BF16)
    w2_all = jnp.concatenate([w2_hi, w2_lo, h2_all], axis=0)
    last = jnp.transpose(jnp.broadcast_to(head_mix[2], (128, CH)))
    last = jnp.concatenate([last, last], axis=1)

    lf = []
    for l in range(3):
        weight = jnp.concatenate([cur_in[l][:, :NF], old_in[l][:, :NF]], axis=1)
        if l == 0:
            top = jnp.concatenate([head_in[:, :NF], jnp.zeros((1, NF), F32)], axis=1)
            weight = jnp.concatenate([weight, jnp.broadcast_to(top, (8, 2 * NF))], axis=0)
        hi = weight.astype(BF16).astype(F32)
        lf.append(jnp.concatenate([hi, weight - hi], axis=1).astype(BF16))

    def theta_weight(x):
        x = jnp.concatenate([x[:, NF:], jnp.zeros((x.shape[0], 8), F32)], axis=1)
        hi = x.astype(BF16).astype(F32)
        return jnp.concatenate([hi, x - hi], axis=1).astype(BF16)

    theta_weights = []
    for l in range(3):
        theta_weights.append(theta_weight(cur_in[l]))
        theta_weights.append(theta_weight(cur_in[l] + old_in[l]))
    theta_weights.append(theta_weight(jnp.broadcast_to(head_in, (8, 32))))

    for k in range(1, 4):
        source = (x_at + k) % 4
        remote(
            near.at[source], near.at[source], near_send.at[k], near_recv.at[source], x_peer(k)
        ).wait_recv()
    merged[...] = (near[0] + near[1]) + (near[2] + near[3])

    def far_copy(k):
        where = far_target(k)[2]
        return remote(
            far_message.at[k], pars.at[z_high], far_send.at[k], far_recv.at[z_high], where
        )

    for k in range(4):
        wanted_region, wanted_crop, where = far_target(k)
        wanted_crop = wanted_crop % n_crop
        for a in range(MSUB):
            far_message[k, a, 0:1, :] = merged[a, pl.ds(wanted_region, 1), :]
            far_message[k, a, 1:2, :] = merged[a, pl.ds(wanted_crop, 1), :]
        if k < 2:
            far_copy(k).start()
        else:

            @pl.when(inside)
            def _():
                far_copy(k).start()

    for a in range(MSUB):
        pars[z_high, a, 0:1, :] = merged[a, pl.ds(region, 1), :]
        pars[z_high, a, 1:2, :] = merged[a, pl.ds(crop, 1), :]

    for copy in copies:
        copy.wait_recv()
    for a in range(MSUB):
        for k in range(SLOTS // HALF):
            at = a * SLOTS + k * HALF
            stacked[at : at + HALF, :] = got[k]
    ft[: PAD * NF, :] = jnp.zeros((PAD * NF, LANES), F32)
    ft[PAD * NF :, :] = jnp.transpose(stacked[...])

    def several(body, count):
        def step(i, carry):
            for d in range(count):
                body(i * count + d)
            return carry

        lax.fori_loop(0, WEEKS // count, step, 0)

    def forcing_part(t):
        now = ft[pl.ds((t + PAD) * NF, NF), :]
        for l in range(3):
            late = ft[pl.ds((t + PAD - 2**l) * NF, NF), :]
            x = jnp.concatenate([now, late, now, late], axis=0).astype(BF16)
            y = dot(lf[l], x)
            if l == 0:
                fpart[t, 3 * CH : 3 * CH + 8, :] = y[CH:, :]
            fpart[t, l * CH : (l + 1) * CH, :] = y[:CH, :]

    several(forcing_part, 13)
    inner0[:PAD] = jnp.zeros((PAD, CH, width), BF16)
    inner1[:PAD] = jnp.zeros((PAD, CH, width), BF16)

    for k in range(1, 4):
        high, where = far_source(k)
        remote(
            far_message.at[0], pars.at[high], far_send.at[0], far_recv.at[high], where
        ).wait_recv()
    for h in range(4):
        for a in range(MSUB):
            theta_rows[h * MSUB + a : h * MSUB + a + 1, :] = pars[h, a, 0:1, :]
    theta = theta_rows[...].astype(BF16)
    lane_of = iota((16, 512), 1) // SLOTS == iota((16, 512), 0)
    lane_of = jnp.where(lane_of, 1.0, 0.0).astype(BF16)
    theta_wide = jnp.concatenate(
        [tn(theta[:, 32 * q : 32 * (q + 1)], lane_of) for q in range(4)], axis=1
    )
    theta_twice = jnp.concatenate([theta_wide, theta_wide], axis=0).astype(BF16)
    for l in range(6):
        gpart[l] = dot(theta_weights[l], theta_twice)
    ghead[...] = dot(theta_weights[6], theta_twice)

    def twice(x):
        return jnp.concatenate([x, x], axis=1)

    def layer01(t):
        g0 = jnp.where(t >= 1, 1, 0)
        g1 = jnp.where(t >= 2, 3, 2)
        f = fpart[t]
        for j in range(tiles):
            at = pl.ds(j * 256, 256)
            x0 = jnp.maximum(twice(f[:CH]) + gpart[g0, :, at], 0.0).astype(BF16)
            inner0[t + PAD, :, at] = x0
            x = jnp.concatenate([x0, inner0[t + PAD - 2, :, at]], axis=0)
            y = dot(w1_all, x)
            y = y[:CH] + y[CH:] + (twice(f[CH : 2 * CH]) + gpart[g1, :, at])
            inner1[t + PAD, :, at] = jnp.maximum(y, 0.0).astype(BF16)

    several(layer01, 4)

    def layer2(t):
        g2 = jnp.where(t >= 4, 5, 4)
        f = fpart[t]
        for j in range(tiles):
            at = pl.ds(j * 256, 256)
            x = jnp.concatenate(
                [
                    inner0[t + PAD, :, at],
                    inner0[t + PAD - 4, :, at],
                    inner1[t + PAD, :, at],
                    inner1[t + PAD - 4, :, at],
                ],
                axis=0,
            )
            y = dot(w2_all, x)
            z = y[:CH] + y[CH : 2 * CH] + (twice(f[2 * CH : 3 * CH]) + gpart[g2, :, at])
            z = jnp.maximum(z, 0.0) * last
            line = jnp.sum(z, axis=0, keepdims=True)
            line = line + y[2 * CH : 2 * CH + 1] + y[2 * CH + 1 : 2 * CH + 2]
            line = line + twice(f[3 * CH : 3 * CH + 1]) + ghead[:1, at]
            pred[t, 2 * j : 2 * j + 1, :] = line[:, :LANES]
            pred[t, 2 * j + 1 : 2 * j + 2, :] = line[:, LANES:]

    several(layer2, 4)

    p = pred[...]
    total = jnp.sum(p, axis=1)
    total = total + pltpu.roll(total, 2 * SLOTS, 1)
    total = total + pltpu.roll(total, SLOTS, 1)
    mean = total / members
    base = PAD * NF
    obs = ft[base + OBS_AT : base + OBS_AT + WEEKS, :]
    wgt = ft[base + WGT_AT : base + WGT_AT + WEEKS, :]
    innovation = wgt * (obs - mean) / math.sqrt(ALPHA_INFLATION)
    factor = wgt / math.sqrt(ALPHA_INFLATION * (members - 1))
    pred[...] = (p - mean[:, None, :]) * factor[:, None, :]

    block = iota((groups, LANES), 1) // SLOTS
    ext[members:, :] = jnp.zeros((ext.shape[0] - members, ext.shape[1]), BF16)
    block8 = iota((8, LANES), 1) // SLOTS
    row8 = iota((8, LANES), 0)
    for q in range(WEEKS // MSUB):
        weeks = [pred[MSUB * q + b] for b in range(MSUB)]
        parts = []
        for a in range(MSUB):
            turned = weeks[a]
            for b in range(MSUB):
                if b != a:
                    moved = pltpu.roll(weeks[b], (b - a) % MSUB * SLOTS, 1)
                    turned = jnp.where(block == b, moved, turned)
            parts.append(turned)
        cols = slice(LANES * q, LANES * (q + 1))
        ext[:members, cols] = jnp.concatenate(parts, axis=0).astype(BF16)
        inn = jnp.zeros((8, LANES), F32)
        for b in range(MSUB):
            line = jnp.broadcast_to(innovation[MSUB * q + b : MSUB * q + b + 1], (8, LANES))
            inn = jnp.where(block8 == b, line, inn)
        hi = inn.astype(BF16).astype(F32)
        inn = jnp.where(row8 == 0, hi, jnp.where(row8 == 1, inn - hi, 0.0))
        inn = jnp.concatenate([inn, jnp.zeros((8, LANES), F32)], axis=0)
        ext[members : members + 16, cols] = inn.astype(BF16)
    gram[...] = nt(ext[:members, :], ext[...]).reshape(n_crop, 8, 128)

    sums = []
    for k in range(1, n_crop):
        where = crop_peer(k)
        copy = remote(gram.at[where["crop"]], part.at[k], send_a.at[k], recv_a.at[k], where)
        copy.start()
        sums.append(copy)

    for h in range(4):
        for a in range(MSUB):
            theta_rows[h * MSUB + a : h * MSUB + a + 1, :] = pars[h, a, 1:2, :]
    theta = theta_rows[...]
    for q in range(4):
        turned = pltpu.roll(theta, (4 - q) % 4 * 32, 1) if q else theta
        for h in range(4):
            for a in range(MSUB):
                at = a * groups + q * 4 + h
                spread_rows[at : at + 1, :] = turned[h * MSUB + a : h * MSUB + a + 1, :]
    lane = iota((members, 128), 1)
    row = iota((members, 128), 0)
    theta = jnp.where(lane < NP, spread_rows[...], 0.0)
    centre = jnp.sum(theta, axis=0, keepdims=True) / members
    spread = (theta - centre) / math.sqrt(members - 1)

    acc = gram[crop]
    for copy in sums:
        copy.wait_recv()
    for k in range(1, n_crop):
        acc = acc + part[k]
    one[0] = acc
    adds = []
    for k in range(1, peers):
        q, where = sum_peer(k)
        copy = remote(one.at[0], every.at[mine], send_b.at[k], recv_b.at[mine], where)
        copy.start()
        adds.append(copy)
    every[mine] = acc
    for k in range(1, peers):
        q, where = sum_peer(k)
        remote(one.at[0], every.at[q], send_b.at[k], recv_b.at[q], where).wait_recv()
    acc = every[0]
    for q in range(1, peers):
        acc = acc + every[q]
    one[1] = acc

    beside = (x_at + jnp.where(half == 0, 3, 1)) % 4

    def row_copy(k):
        to_x = x_at if k < 4 else beside
        where = {"crop": region, "member": to_x * 4 + (z_high + k) % 4}
        return remote(one.at[1], final.at[crop], send_c.at[k], recv_c.at[crop], where)

    away = region != crop
    for k in (2, 6, 1, 3, 5, 7, 4):
        row_copy(k).start()

    @pl.when(away)
    def _():
        row_copy(0).start()

    @pl.when(jnp.logical_not(away))
    def _():
        final[crop] = one[1]

    from_x = jnp.where(x_at // 2 == crop % 2, x_at, beside)

    def row_arrival(source):
        where = {"crop": source, "member": from_x * 4 + crop // 2}
        return remote(one.at[1], final.at[source], send_c.at[0], recv_c.at[source], where)

    for k in range(1, n_crop):
        row_arrival((crop + k) % n_crop).wait_recv()

    @pl.when(away)
    def _():
        row_arrival(crop).wait_recv()

    whole = final[...].reshape(members, 128)
    proj = whole[:, members : members + 1] + whole[:, members + 1 : members + 2]
    moved = pltpu.roll(spread, members, 1)
    system = jnp.where(lane < members, whole + jnp.where(lane == row, 1.0, 0.0), moved)
    for k in range(members):
        line = system[k : k + 1, :]
        line = line / line[:, k : k + 1]
        column = system[:, k : k + 1]
        factor = jnp.broadcast_to(column, (members, 128)) - jnp.where(row == k, 1.0, 0.0)
        system = system - factor * line
    y = jnp.where(lane >= members, system, 0.0)
    y = pltpu.roll(y, 128 - members, 1)
    solved[...] = y
    shared = centre + jnp.sum(proj * y, axis=0, keepdims=True)
    for a in range(MSUB):
        own = solved[pl.ds(a * groups + member, 1), :]
        result = shared + math.sqrt(members - 1) * own
        out[a] = result[:, :NP]

    for copy in near_copies + sums + adds:
        copy.wait_send()
    for copy in copies:
        copy.wait_send()
    for k in range(4):
        if k < 2:
            far_copy(k).wait_send()
        else:

            @pl.when(inside)
            def _():
                far_copy(k).wait_send()

    for k in range(1, 8):
        row_copy(k).wait_send()

    @pl.when(away)
    def _():
        row_copy(0).wait_send()


def local(
    sizes,
    forcing, observed, obs_sigma, pixel_class, pixel_count, cloud_free, params,
    input_weight, conv_weight, mix_weight, head_weight,
):
    n_pixel, n_crop, n_member = sizes
    pixels = obs_sigma.shape[0]
    members = params.shape[0] * n_member
    groups = members // MSUB
    width = groups * LANES
    args = (
        forcing, observed, obs_sigma, pixel_class.reshape(1, pixels), pixel_count, cloud_free,
        params, jnp.swapaxes(input_weight, 1, 2), conv_weight, mix_weight, head_weight,
    )
    anywhere = pl.BlockSpec(memory_space=pl.ANY)
    vmem = pl.BlockSpec(memory_space=pltpu.VMEM)
    smem = pl.BlockSpec(memory_space=pltpu.SMEM)
    dma = pltpu.SemaphoreType.DMA
    copies = [pltpu.VMEM(a.shape, a.dtype) for i, a in enumerate(args) if i != 4]
    return pl.pallas_call(
        functools.partial(mega_kernel, n_pixel, n_crop),
        name="smoother",
        out_shape=jax.ShapeDtypeStruct((MSUB, 1, NP), F32),
        in_specs=[smem if i == 4 else anywhere for i in range(len(args))],
        out_specs=vmem,
        scratch_shapes=copies + [
            pltpu.VMEM((ROW, pixels), F32),
            pltpu.VMEM((n_crop, HALF, ROW), F32),
            pltpu.VMEM((n_crop, HALF, ROW), F32),
            pltpu.VMEM((4, MSUB, 8, 128), F32),
            pltpu.VMEM((MSUB, 8, 128), F32),
            pltpu.VMEM((4, MSUB, 2, 128), F32),
            pltpu.VMEM((4, MSUB, 2, 128), F32),
            pltpu.VMEM((16, 128), F32),
            pltpu.VMEM((LANES, ROW), F32),
            pltpu.VMEM((PAD * NF + ROW, LANES), F32),
            pltpu.VMEM((WEEKS, 3 * CH + 8, LANES), F32),
            pltpu.VMEM((6, CH, width), F32),
            pltpu.VMEM((8, width), F32),
            pltpu.VMEM((PAD + WEEKS, CH, width), BF16),
            pltpu.VMEM((PAD + WEEKS, CH, width), BF16),
            pltpu.VMEM((WEEKS, groups, LANES), F32),
            pltpu.VMEM((128, WEEKS // MSUB * LANES), BF16),
            pltpu.VMEM((n_crop, 8, 128), F32),
            pltpu.VMEM((n_crop, 8, 128), F32),
            pltpu.VMEM((2, 8, 128), F32),
            pltpu.VMEM((2 * n_pixel, 8, 128), F32),
            pltpu.VMEM((n_crop, 8, 128), F32),
            pltpu.VMEM((members, 128), F32),
            pltpu.VMEM((members, 128), F32),
            dma((10,)), dma((n_crop,)), dma((n_crop,)), dma((4,)), dma((4,)), dma((4,)), dma((4,)),
            dma((n_crop,)), dma((n_crop,)), dma((2 * n_pixel,)), dma((2 * n_pixel,)),
            dma((8,)), dma((n_crop,)),
        ],
        compiler_params=pltpu.CompilerParams(
            collective_id=0, has_side_effects=True, vmem_limit_bytes=(64 << 20) - 4096
        ),
    )(*args)


def solution(mesh):
    sizes = (mesh.shape["pixel"], mesh.shape["crop"], mesh.shape["member"])
    in_specs = (
        P(None, None, ("pixel", "crop")),
        P(None, ("pixel", "crop")),
        P(("pixel", "crop")),
        P(("pixel", "crop"), None),
        P(("pixel", "crop")),
        P(("pixel", "crop"), None),
        P("member", None, None),
        P("crop", None, None),
        P("crop", None, None, None),
        P("crop", None, None, None),
        P("crop", None),
    )
    return jax.shard_map(
        functools.partial(local, sizes),
        mesh=mesh,
        in_specs=in_specs,
        out_specs=P("member", "crop", None),
        check_vma=False,
    )
```

```python
import functools
import math

import jax
import jax.numpy as jnp
from jax import lax
from jax.experimental import pallas as pl
from jax.experimental.pallas import tpu as pltpu
from jax.sharding import PartitionSpec as P

MESH = pl.DeviceIdType.MESH
F32 = jnp.float32
BF16 = jnp.bfloat16
WEEKS = 52
CH = 48
NF = 8
NP = 24
CAP = 8
BLK = 32
ALPHA_INFLATION = 4.0
HALF = CAP // 2
SLOTS = 32
MSUB = 4
LANES = MSUB * SLOTS
ROW = 640
OBS_AT = 512
WGT_AT = 576
PAD = 4


def iota(shape, dim):
    return lax.broadcasted_iota(jnp.int32, shape, dim)


def nt(a, b):
    return lax.dot_general(a, b, (((1,), (1,)), ((), ())), preferred_element_type=F32)


def tn(a, b):
    return lax.dot_general(a, b, (((0,), (0,)), ((), ())), preferred_element_type=F32)


def hi_lo(x):
    hi = x.astype(BF16)
    return hi, (x - hi.astype(F32)).astype(BF16)


def mega_kernel(
    n_pixel, n_crop,
    forcing_hbm, observed_hbm, sigma_hbm, classes_hbm, counts, cloud_hbm, params_hbm,
    input_hbm, conv_hbm, mix_hbm, head_hbm,
    out,
    forcing, observed, sigma, classes, cloud, params, input_weight, conv_weight, mix_weight,
    head_weight,
    rows, message, got, near, merged, far_message, pars, theta_rows,
    stacked, ft, fpart, gpart, ghead, inner0, inner1, pred, ext,
    gram, part, one, every, final, spread_rows, solved,
    load, send, recv, near_send, near_recv, far_send, far_recv,
    send_a, recv_a, send_b, recv_b, send_c, recv_c,
):
    pixel = lax.axis_index("pixel")
    crop = lax.axis_index("crop")
    member = lax.axis_index("member")
    x_at = member // 4
    z_high = member % 4
    z_low = crop // 2
    core = crop % 2
    region = z_high * 2 + x_at // 2
    half = x_at % 2
    pixels = rows.shape[1]
    blocks = cloud.shape[0]
    peers = 2 * n_pixel
    mine = pixel * 2 + half
    members = spread_rows.shape[0]
    groups = members // MSUB
    width = groups * LANES
    tiles = width // 256

    def dot(a, b):
        return jnp.dot(a, b, preferred_element_type=F32)

    def remote(src, dst, send_sem, recv_sem, where):
        return pltpu.make_async_remote_copy(
            src_ref=src, dst_ref=dst, send_sem=send_sem, recv_sem=recv_sem,
            device_id=where, device_id_type=MESH,
        )

    loads = []
    pairs = (
        (params_hbm, params), (forcing_hbm, forcing), (observed_hbm, observed),
        (sigma_hbm, sigma), (classes_hbm, classes), (cloud_hbm, cloud),
        (input_hbm, input_weight), (conv_hbm, conv_weight), (mix_hbm, mix_weight),
        (head_hbm, head_weight),
    )
    for i, (src, dst) in enumerate(pairs):
        copy = pltpu.make_async_copy(src, dst, load.at[i])
        copy.start()
        loads.append(copy)

    def crop_peer(k):
        return {"crop": (crop + k) % n_crop}

    def x_peer(k):
        return {"member": (x_at + k) % 4 * 4 + z_high}

    def sum_peer(k):
        q = (mine + k) % peers
        return q, {"pixel": q // 2, "member": (x_at // 2 * 2 + q % 2) * 4 + z_high}

    inside = (z_low == 1) | (z_low == 2)
    slab = jnp.where(z_low == 2, 1, jnp.where(z_low == 1, 3, 2))

    def far_target(k):
        z_to = k + jnp.where(z_low == 0, 2, 0)
        high = (z_high + slab) % 4
        return high * 2 + x_at // 2, z_to * 2 + core, {
            "crop": z_to * 2 + core, "member": x_at * 4 + high
        }

    def far_source(k):
        z_from = (1, jnp.where(z_low < 2, 3, 0), 2)[k - 1]
        high = (z_high + k) % 4
        return high, {"crop": z_from * 2 + core, "member": x_at * 4 + high}

    barrier = pltpu.get_barrier_semaphore()
    for k in range(1, 4):
        pl.semaphore_signal(barrier, inc=1, device_id=far_source(k)[1], device_id_type=MESH)
    for k in range(1, n_crop):
        pl.semaphore_signal(barrier, inc=1, device_id=crop_peer(k), device_id_type=MESH)
    for k in range(1, 4):
        pl.semaphore_signal(barrier, inc=1, device_id=x_peer(k), device_id_type=MESH)
    for k in range(1, peers):
        pl.semaphore_signal(barrier, inc=1, device_id=sum_peer(k)[1], device_id_type=MESH)

    loads[0].wait()
    quarter = iota((8, 128), 1) // 32
    for a in range(MSUB):
        block = jnp.concatenate([params[a], jnp.zeros((8, 32 - NP), F32)], axis=1)
        block = jnp.concatenate([block] * 4, axis=1)
        near[x_at, a] = jnp.where(quarter == x_at, block, 0.0)

    for copy in loads[1:6]:
        copy.wait()
    place = iota((1, pixels), 1)
    limit = jnp.zeros((1, pixels), jnp.int32)
    for b in range(blocks):
        limit = jnp.where(place // BLK == b, counts[b], limit)
    live = place % BLK < limit
    slots = n_crop * HALF
    slot = iota((slots, pixels), 0)
    named = (classes[...] == (slot // HALF) * 8 + region) & live
    named = jnp.where(named, 1.0, 0.0)
    before = jnp.where(iota((pixels, pixels), 0) < iota((pixels, pixels), 1), 1.0, 0.0)
    rank = dot(named.astype(BF16), before.astype(BF16))
    wanted = (slot % HALF + half * HALF).astype(F32)
    select = jnp.where(rank == wanted, named, 0.0).astype(BF16)

    in_block = iota((blocks, pixels), 1) // BLK == iota((blocks, pixels), 0)
    seen = tn(cloud[...].astype(F32).astype(BF16), jnp.where(in_block, 1.0, 0.0).astype(BF16))
    rows[...] = jnp.zeros_like(rows)
    rows[: WEEKS * NF, :] = forcing[...].astype(F32).reshape(WEEKS * NF, pixels)
    rows[OBS_AT : OBS_AT + WEEKS, :] = observed[...].astype(F32)
    rows[WGT_AT : WGT_AT + WEEKS, :] = seen / sigma[...].reshape(1, pixels)
    packed = nt(select, rows[...].astype(BF16))
    for c in range(n_crop):
        message[c] = packed[HALF * c : HALF * (c + 1), :]

    pl.semaphore_wait(barrier, 3 + n_crop - 1 + peers - 1 + jnp.where(inside, 4, 2))
    near_copies = [
        remote(near.at[x_at], near.at[x_at], near_send.at[k], near_recv.at[x_at], x_peer(k))
        for k in range(1, 4)
    ]
    for copy in near_copies:
        copy.start()
    copies = []
    for k in range(1, n_crop):
        where = crop_peer(k)
        copy = remote(message.at[where["crop"]], got.at[k], send.at[k], recv.at[k], where)
        copy.start()
        copies.append(copy)
    got[0] = message[crop]

    for copy in loads[6:]:
        copy.wait()
    mixes = [mix_weight[0, l] for l in range(3)]
    convs = [conv_weight[0, l] for l in range(3)]
    cur = [c[:, :CH] for c in convs]
    old = [c[:, CH:] for c in convs]
    head = head_weight[...]
    w_in = input_weight[0]
    cur_in = [nt(a, w_in) for a in cur]
    old_in = [nt(a, w_in) for a in old]
    head_in = nt(head, w_in)
    w1 = jnp.concatenate([dot(cur[1], mixes[0]), dot(old[1], mixes[0])], axis=1)
    w2 = jnp.concatenate(
        [
            dot(cur[2], mixes[0]),
            dot(old[2], mixes[0]),
            dot(cur[2], mixes[1]),
            dot(old[2], mixes[1]),
        ],
        axis=1,
    )
    head_mix = [dot(head, m) for m in mixes]
    zero_row = jnp.zeros((1, CH), F32)
    head2 = jnp.concatenate([head_mix[0], zero_row, head_mix[1], zero_row], axis=1)
    w1_hi, w1_lo = hi_lo(w1)
    w1_all = jnp.concatenate([w1_hi, w1_lo], axis=0)
    w2_hi, w2_lo = hi_lo(w2)
    h2_hi, h2_lo = hi_lo(jnp.broadcast_to(head2, (16, 4 * CH)))
    h2_all = jnp.where(
        iota((16, 4 * CH), 0) == 0,
        h2_hi.astype(F32),
        jnp.where(iota((16, 4 * CH), 0) == 1, h2_lo.astype(F32), 0.0),
    ).astype(BF16)
    w2_all = jnp.concatenate([w2_hi, w2_lo, h2_all], axis=0)
    last = jnp.transpose(jnp.broadcast_to(head_mix[2], (128, CH)))
    last = jnp.concatenate([last, last], axis=1)

    lf = []
    for l in range(3):
        weight = jnp.concatenate([cur_in[l][:, :NF], old_in[l][:, :NF]], axis=1)
        if l == 0:
            top = jnp.concatenate([head_in[:, :NF], jnp.zeros((1, NF), F32)], axis=1)
            weight = jnp.concatenate([weight, jnp.broadcast_to(top, (8, 2 * NF))], axis=0)
        hi = weight.astype(BF16).astype(F32)
        lf.append(jnp.concatenate([hi, weight - hi], axis=1).astype(BF16))

    def theta_weight(x):
        x = jnp.concatenate([x[:, NF:], jnp.zeros((x.shape[0], 8), F32)], axis=1)
        hi = x.astype(BF16).astype(F32)
        return jnp.concatenate([hi, x - hi], axis=1).astype(BF16)

    theta_weights = []
    for l in range(3):
        theta_weights.append(theta_weight(cur_in[l]))
        theta_weights.append(theta_weight(cur_in[l] + old_in[l]))
    theta_weights.append(theta_weight(jnp.broadcast_to(head_in, (8, 32))))

    for k in range(1, 4):
        source = (x_at + k) % 4
        remote(
            near.at[source], near.at[source], near_send.at[k], near_recv.at[source], x_peer(k)
        ).wait_recv()
    merged[...] = (near[0] + near[1]) + (near[2] + near[3])

    def far_copy(k):
        where = far_target(k)[2]
        return remote(
            far_message.at[k], pars.at[z_high], far_send.at[k], far_recv.at[z_high], where
        )

    for k in range(4):
        wanted_region, wanted_crop, where = far_target(k)
        wanted_crop = wanted_crop % n_crop
        for a in range(MSUB):
            far_message[k, a, 0:1, :] = merged[a, pl.ds(wanted_region, 1), :]
            far_message[k, a, 1:2, :] = merged[a, pl.ds(wanted_crop, 1), :]
        if k < 2:
            far_copy(k).start()
        else:

            @pl.when(inside)
            def _():
                far_copy(k).start()

    for a in range(MSUB):
        pars[z_high, a, 0:1, :] = merged[a, pl.ds(region, 1), :]
        pars[z_high, a, 1:2, :] = merged[a, pl.ds(crop, 1), :]

    for copy in copies:
        copy.wait_recv()
    for a in range(MSUB):
        for k in range(SLOTS // HALF):
            at = a * SLOTS + k * HALF
            stacked[at : at + HALF, :] = got[k]
    ft[: PAD * NF, :] = jnp.zeros((PAD * NF, LANES), F32)
    ft[PAD * NF :, :] = jnp.transpose(stacked[...])

    def several(body, count):
        def step(i, carry):
            for d in range(count):
                body(i * count + d)
            return carry

        lax.fori_loop(0, WEEKS // count, step, 0)

    def forcing_part(t):
        now = ft[pl.ds((t + PAD) * NF, NF), :]
        for l in range(3):
            late = ft[pl.ds((t + PAD - 2**l) * NF, NF), :]
            x = jnp.concatenate([now, late, now, late], axis=0).astype(BF16)
            y = dot(lf[l], x)
            if l == 0:
                fpart[t, 3 * CH : 3 * CH + 8, :] = y[CH:, :]
            fpart[t, l * CH : (l + 1) * CH, :] = y[:CH, :]

    several(forcing_part, 13)
    inner0[:PAD] = jnp.zeros((PAD, CH, width), BF16)
    inner1[:PAD] = jnp.zeros((PAD, CH, width), BF16)

    for k in range(1, 4):
        high, where = far_source(k)
        remote(
            far_message.at[0], pars.at[high], far_send.at[0], far_recv.at[high], where
        ).wait_recv()
    for h in range(4):
        for a in range(MSUB):
            theta_rows[h * MSUB + a : h * MSUB + a + 1, :] = pars[h, a, 0:1, :]
    theta = theta_rows[...].astype(BF16)
    lane_of = iota((16, 512), 1) // SLOTS == iota((16, 512), 0)
    lane_of = jnp.where(lane_of, 1.0, 0.0).astype(BF16)
    theta_wide = jnp.concatenate(
        [tn(theta[:, 32 * q : 32 * (q + 1)], lane_of) for q in range(4)], axis=1
    )
    theta_twice = jnp.concatenate([theta_wide, theta_wide], axis=0).astype(BF16)
    for l in range(6):
        gpart[l] = dot(theta_weights[l], theta_twice)
    ghead[...] = dot(theta_weights[6], theta_twice)

    def twice(x):
        return jnp.concatenate([x, x], axis=1)

    zero16 = jnp.zeros((CH, 256), BF16)

    def layer01(t):
        g0 = jnp.where(t >= 1, 1, 0)
        g1 = jnp.where(t >= 2, 3, 2)
        f = fpart[t]
        for j in range(tiles):
            at = pl.ds(j * 256, 256)
            x0 = jnp.maximum((twice(f[:CH]) + gpart[g0, :, at]).astype(BF16), zero16)
            inner0[t + PAD, :, at] = x0
            x = jnp.concatenate([x0, inner0[t + PAD - 2, :, at]], axis=0)
            y = dot(w1_all, x)
            y = y[:CH] + y[CH:] + (twice(f[CH : 2 * CH]) + gpart[g1, :, at])
            inner1[t + PAD, :, at] = jnp.maximum(y.astype(BF16), zero16)

    several(layer01, 13)

    def layer2(t):
        g2 = jnp.where(t >= 4, 5, 4)
        f = fpart[t]
        for j in range(tiles):
            at = pl.ds(j * 256, 256)
            x = jnp.concatenate(
                [
                    inner0[t + PAD, :, at],
                    inner0[t + PAD - 4, :, at],
                    inner1[t + PAD, :, at],
                    inner1[t + PAD - 4, :, at],
                ],
                axis=0,
            )
            y = dot(w2_all, x)
            z = y[:CH] + y[CH : 2 * CH] + (twice(f[2 * CH : 3 * CH]) + gpart[g2, :, at])
            z = jnp.maximum(z, 0.0) * last
            line = jnp.sum(z, axis=0, keepdims=True)
            line = line + y[2 * CH : 2 * CH + 1] + y[2 * CH + 1 : 2 * CH + 2]
            line = line + twice(f[3 * CH : 3 * CH + 1]) + ghead[:1, at]
            pred[t, 2 * j : 2 * j + 1, :] = line[:, :LANES]
            pred[t, 2 * j + 1 : 2 * j + 2, :] = line[:, LANES:]

    several(layer2, 13)

    p = pred[...]
    total = jnp.sum(p, axis=1)
    total = total + pltpu.roll(total, 2 * SLOTS, 1)
    total = total + pltpu.roll(total, SLOTS, 1)
    mean = total / members
    base = PAD * NF
    obs = ft[base + OBS_AT : base + OBS_AT + WEEKS, :]
    wgt = ft[base + WGT_AT : base + WGT_AT + WEEKS, :]
    innovation = wgt * (obs - mean) / math.sqrt(ALPHA_INFLATION)
    factor = wgt / math.sqrt(ALPHA_INFLATION * (members - 1))
    pred[...] = (p - mean[:, None, :]) * factor[:, None, :]

    block = iota((groups, LANES), 1) // SLOTS
    ext[members:, :] = jnp.zeros((ext.shape[0] - members, ext.shape[1]), BF16)
    block8 = iota((8, LANES), 1) // SLOTS
    row8 = iota((8, LANES), 0)
    for q in range(WEEKS // MSUB):
        weeks = [pred[MSUB * q + b] for b in range(MSUB)]
        parts = []
        for a in range(MSUB):
            turned = weeks[a]
            for b in range(MSUB):
                if b != a:
                    moved = pltpu.roll(weeks[b], (b - a) % MSUB * SLOTS, 1)
                    turned = jnp.where(block == b, moved, turned)
            parts.append(turned)
        cols = slice(LANES * q, LANES * (q + 1))
        ext[:members, cols] = jnp.concatenate(parts, axis=0).astype(BF16)
        inn = jnp.zeros((8, LANES), F32)
        for b in range(MSUB):
            line = jnp.broadcast_to(innovation[MSUB * q + b : MSUB * q + b + 1], (8, LANES))
            inn = jnp.where(block8 == b, line, inn)
        hi = inn.astype(BF16).astype(F32)
        inn = jnp.where(row8 == 0, hi, jnp.where(row8 == 1, inn - hi, 0.0))
        inn = jnp.concatenate([inn, jnp.zeros((8, LANES), F32)], axis=0)
        ext[members : members + 16, cols] = inn.astype(BF16)
    gram[...] = nt(ext[:members, :], ext[...]).reshape(n_crop, 8, 128)

    sums = []
    for k in range(1, n_crop):
        where = crop_peer(k)
        copy = remote(gram.at[where["crop"]], part.at[k], send_a.at[k], recv_a.at[k], where)
        copy.start()
        sums.append(copy)

    for h in range(4):
        for a in range(MSUB):
            theta_rows[h * MSUB + a : h * MSUB + a + 1, :] = pars[h, a, 1:2, :]
    theta = theta_rows[...]
    for q in range(4):
        turned = pltpu.roll(theta, (4 - q) % 4 * 32, 1) if q else theta
        for h in range(4):
            for a in range(MSUB):
                at = a * groups + q * 4 + h
                spread_rows[at : at + 1, :] = turned[h * MSUB + a : h * MSUB + a + 1, :]
    lane = iota((members, 128), 1)
    row = iota((members, 128), 0)
    theta = jnp.where(lane < NP, spread_rows[...], 0.0)
    centre = jnp.sum(theta, axis=0, keepdims=True) / members
    spread = (theta - centre) / math.sqrt(members - 1)

    acc = gram[crop]
    for copy in sums:
        copy.wait_recv()
    for k in range(1, n_crop):
        acc = acc + part[k]
    one[0] = acc
    adds = []
    for k in range(1, peers):
        q, where = sum_peer(k)
        copy = remote(one.at[0], every.at[mine], send_b.at[k], recv_b.at[mine], where)
        copy.start()
        adds.append(copy)
    every[mine] = acc
    for k in range(1, peers):
        q, where = sum_peer(k)
        remote(one.at[0], every.at[q], send_b.at[k], recv_b.at[q], where).wait_recv()
    acc = every[0]
    for q in range(1, peers):
        acc = acc + every[q]
    one[1] = acc

    beside = (x_at + jnp.where(half == 0, 3, 1)) % 4

    def row_copy(k):
        to_x = x_at if k < 4 else beside
        where = {"crop": region, "member": to_x * 4 + (z_high + k) % 4}
        return remote(one.at[1], final.at[crop], send_c.at[k], recv_c.at[crop], where)

    away = region != crop
    for k in (2, 6, 1, 3, 5, 7, 4):
        row_copy(k).start()

    @pl.when(away)
    def _():
        row_copy(0).start()

    @pl.when(jnp.logical_not(away))
    def _():
        final[crop] = one[1]

    from_x = jnp.where(x_at // 2 == crop % 2, x_at, beside)

    def row_arrival(source):
        where = {"crop": source, "member": from_x * 4 + crop // 2}
        return remote(one.at[1], final.at[source], send_c.at[0], recv_c.at[source], where)

    for k in range(1, n_crop):
        row_arrival((crop + k) % n_crop).wait_recv()

    @pl.when(away)
    def _():
        row_arrival(crop).wait_recv()

    whole = final[...].reshape(members, 128)
    proj = whole[:, members : members + 1] + whole[:, members + 1 : members + 2]
    moved = pltpu.roll(spread, members, 1)
    system = jnp.where(lane < members, whole + jnp.where(lane == row, 1.0, 0.0), moved)
    for k in range(members):
        line = system[k : k + 1, :]
        line = line / line[:, k : k + 1]
        column = system[:, k : k + 1]
        factor = jnp.broadcast_to(column, (members, 128)) - jnp.where(row == k, 1.0, 0.0)
        system = system - factor * line
    y = jnp.where(lane >= members, system, 0.0)
    y = pltpu.roll(y, 128 - members, 1)
    solved[...] = y
    shared = centre + jnp.sum(proj * y, axis=0, keepdims=True)
    for a in range(MSUB):
        own = solved[pl.ds(a * groups + member, 1), :]
        result = shared + math.sqrt(members - 1) * own
        out[a] = result[:, :NP]

    for copy in near_copies + sums + adds:
        copy.wait_send()
    for copy in copies:
        copy.wait_send()
    for k in range(4):
        if k < 2:
            far_copy(k).wait_send()
        else:

            @pl.when(inside)
            def _():
                far_copy(k).wait_send()

    for k in range(1, 8):
        row_copy(k).wait_send()

    @pl.when(away)
    def _():
        row_copy(0).wait_send()


def local(
    sizes,
    forcing, observed, obs_sigma, pixel_class, pixel_count, cloud_free, params,
    input_weight, conv_weight, mix_weight, head_weight,
):
    n_pixel, n_crop, n_member = sizes
    pixels = obs_sigma.shape[0]
    members = params.shape[0] * n_member
    groups = members // MSUB
    width = groups * LANES
    args = (
        forcing, observed, obs_sigma, pixel_class.reshape(1, pixels), pixel_count, cloud_free,
        params, jnp.swapaxes(input_weight, 1, 2), conv_weight, mix_weight, head_weight,
    )
    anywhere = pl.BlockSpec(memory_space=pl.ANY)
    vmem = pl.BlockSpec(memory_space=pltpu.VMEM)
    smem = pl.BlockSpec(memory_space=pltpu.SMEM)
    dma = pltpu.SemaphoreType.DMA
    copies = [pltpu.VMEM(a.shape, a.dtype) for i, a in enumerate(args) if i != 4]
    return pl.pallas_call(
        functools.partial(mega_kernel, n_pixel, n_crop),
        name="smoother",
        out_shape=jax.ShapeDtypeStruct((MSUB, 1, NP), F32),
        in_specs=[smem if i == 4 else anywhere for i in range(len(args))],
        out_specs=vmem,
        scratch_shapes=copies + [
            pltpu.VMEM((ROW, pixels), F32),
            pltpu.VMEM((n_crop, HALF, ROW), F32),
            pltpu.VMEM((n_crop, HALF, ROW), F32),
            pltpu.VMEM((4, MSUB, 8, 128), F32),
            pltpu.VMEM((MSUB, 8, 128), F32),
            pltpu.VMEM((4, MSUB, 2, 128), F32),
            pltpu.VMEM((4, MSUB, 2, 128), F32),
            pltpu.VMEM((16, 128), F32),
            pltpu.VMEM((LANES, ROW), F32),
            pltpu.VMEM((PAD * NF + ROW, LANES), F32),
            pltpu.VMEM((WEEKS, 3 * CH + 8, LANES), F32),
            pltpu.VMEM((6, CH, width), F32),
            pltpu.VMEM((8, width), F32),
            pltpu.VMEM((PAD + WEEKS, CH, width), BF16),
            pltpu.VMEM((PAD + WEEKS, CH, width), BF16),
            pltpu.VMEM((WEEKS, groups, LANES), F32),
            pltpu.VMEM((128, WEEKS // MSUB * LANES), BF16),
            pltpu.VMEM((n_crop, 8, 128), F32),
            pltpu.VMEM((n_crop, 8, 128), F32),
            pltpu.VMEM((2, 8, 128), F32),
            pltpu.VMEM((2 * n_pixel, 8, 128), F32),
            pltpu.VMEM((n_crop, 8, 128), F32),
            pltpu.VMEM((members, 128), F32),
            pltpu.VMEM((members, 128), F32),
            dma((10,)), dma((n_crop,)), dma((n_crop,)), dma((4,)), dma((4,)), dma((4,)), dma((4,)),
            dma((n_crop,)), dma((n_crop,)), dma((2 * n_pixel,)), dma((2 * n_pixel,)),
            dma((8,)), dma((n_crop,)),
        ],
        compiler_params=pltpu.CompilerParams(
            collective_id=0, has_side_effects=True, vmem_limit_bytes=(64 << 20) - 4096
        ),
    )(*args)


def solution(mesh):
    sizes = (mesh.shape["pixel"], mesh.shape["crop"], mesh.shape["member"])
    in_specs = (
        P(None, None, ("pixel", "crop")),
        P(None, ("pixel", "crop")),
        P(("pixel", "crop")),
        P(("pixel", "crop"), None),
        P(("pixel", "crop")),
        P(("pixel", "crop"), None),
        P("member", None, None),
        P("crop", None, None),
        P("crop", None, None, None),
        P("crop", None, None, None),
        P("crop", None),
    )
    return jax.shard_map(
        functools.partial(local, sizes),
        mesh=mesh,
        in_specs=in_specs,
        out_specs=P("member", "crop", None),
        check_vma=False,
    )
```

```python
import functools
import math

import jax
import jax.numpy as jnp
from jax import lax
from jax.experimental import pallas as pl
from jax.experimental.pallas import tpu as pltpu
from jax.sharding import PartitionSpec as P

MESH = pl.DeviceIdType.MESH
F32 = jnp.float32
BF16 = jnp.bfloat16
WEEKS = 52
CH = 48
NF = 8
NP = 24
CAP = 8
BLK = 32
ALPHA_INFLATION = 4.0
HALF = CAP // 2
SLOTS = 32
MSUB = 4
LANES = MSUB * SLOTS
ROW = 640
OBS_AT = 512
WGT_AT = 576
PAD = 4


def iota(shape, dim):
    return lax.broadcasted_iota(jnp.int32, shape, dim)


def nt(a, b):
    return lax.dot_general(a, b, (((1,), (1,)), ((), ())), preferred_element_type=F32)


def tn(a, b):
    return lax.dot_general(a, b, (((0,), (0,)), ((), ())), preferred_element_type=F32)


def hi_lo(x):
    hi = x.astype(BF16)
    return hi, (x - hi.astype(F32)).astype(BF16)


def mega_kernel(
    n_pixel, n_crop,
    forcing_hbm, observed_hbm, sigma_hbm, classes_hbm, counts, cloud_hbm, params_hbm,
    input_hbm, conv_hbm, mix_hbm, head_hbm,
    out,
    forcing, observed, sigma, classes, cloud, params, input_weight, conv_weight, mix_weight,
    head_weight,
    rows, message, got, near, merged, far_message, pars, theta_rows,
    stacked, ft, fpart, gpart, theta_all, w1_all, w2_all, inner0, inner1, pred, ext,
    gram, part, one, every, final, spread_rows, solved,
    load, send, recv, near_send, near_recv, far_send, far_recv,
    send_a, recv_a, send_b, recv_b, send_c, recv_c,
):
    pixel = lax.axis_index("pixel")
    crop = lax.axis_index("crop")
    member = lax.axis_index("member")
    x_at = member // 4
    z_high = member % 4
    z_low = crop // 2
    core = crop % 2
    region = z_high * 2 + x_at // 2
    half = x_at % 2
    pixels = rows.shape[1]
    blocks = cloud.shape[0]
    peers = 2 * n_pixel
    mine = pixel * 2 + half
    members = spread_rows.shape[0]
    groups = members // MSUB
    width = groups * LANES
    tiles = width // 256

    def dot(a, b):
        return jnp.dot(a, b, preferred_element_type=F32)

    def remote(src, dst, send_sem, recv_sem, where):
        return pltpu.make_async_remote_copy(
            src_ref=src, dst_ref=dst, send_sem=send_sem, recv_sem=recv_sem,
            device_id=where, device_id_type=MESH,
        )

    loads = []
    pairs = (
        (params_hbm, params), (forcing_hbm, forcing), (observed_hbm, observed),
        (sigma_hbm, sigma), (classes_hbm, classes), (cloud_hbm, cloud),
        (input_hbm, input_weight), (conv_hbm, conv_weight), (mix_hbm, mix_weight),
        (head_hbm, head_weight),
    )
    for i, (src, dst) in enumerate(pairs):
        copy = pltpu.make_async_copy(src, dst, load.at[i])
        copy.start()
        loads.append(copy)

    def crop_peer(k):
        return {"crop": (crop + k) % n_crop}

    def x_peer(k):
        return {"member": (x_at + k) % 4 * 4 + z_high}

    def sum_peer(k):
        q = (mine + k) % peers
        return q, {"pixel": q // 2, "member": (x_at // 2 * 2 + q % 2) * 4 + z_high}

    inside = (z_low == 1) | (z_low == 2)
    slab = jnp.where(z_low == 2, 1, jnp.where(z_low == 1, 3, 2))

    def far_target(k):
        z_to = k + jnp.where(z_low == 0, 2, 0)
        high = (z_high + slab) % 4
        return high * 2 + x_at // 2, z_to * 2 + core, {
            "crop": z_to * 2 + core, "member": x_at * 4 + high
        }

    def far_source(k):
        z_from = (1, jnp.where(z_low < 2, 3, 0), 2)[k - 1]
        high = (z_high + k) % 4
        return high, {"crop": z_from * 2 + core, "member": x_at * 4 + high}

    barrier = pltpu.get_barrier_semaphore()
    for k in range(1, 4):
        pl.semaphore_signal(barrier, inc=1, device_id=far_source(k)[1], device_id_type=MESH)
    for k in range(1, n_crop):
        pl.semaphore_signal(barrier, inc=1, device_id=crop_peer(k), device_id_type=MESH)
    for k in range(1, 4):
        pl.semaphore_signal(barrier, inc=1, device_id=x_peer(k), device_id_type=MESH)
    for k in range(1, peers):
        pl.semaphore_signal(barrier, inc=1, device_id=sum_peer(k)[1], device_id_type=MESH)

    loads[0].wait()
    quarter = iota((8, 128), 1) // 32
    for a in range(MSUB):
        block = jnp.concatenate([params[a], jnp.zeros((8, 32 - NP), F32)], axis=1)
        block = jnp.concatenate([block] * 4, axis=1)
        near[x_at, a] = jnp.where(quarter == x_at, block, 0.0)

    for copy in loads[1:6]:
        copy.wait()
    place = iota((1, pixels), 1)
    limit = jnp.zeros((1, pixels), jnp.int32)
    for b in range(blocks):
        limit = jnp.where(place // BLK == b, counts[b], limit)
    live = place % BLK < limit
    slots = n_crop * HALF
    slot = iota((slots, pixels), 0)
    named = (classes[...] == (slot // HALF) * 8 + region) & live
    named = jnp.where(named, 1.0, 0.0)
    before = jnp.where(iota((pixels, pixels), 0) < iota((pixels, pixels), 1), 1.0, 0.0)
    rank = dot(named.astype(BF16), before.astype(BF16))
    wanted = (slot % HALF + half * HALF).astype(F32)
    select = jnp.where(rank == wanted, named, 0.0).astype(BF16)

    in_block = iota((blocks, pixels), 1) // BLK == iota((blocks, pixels), 0)
    seen = tn(cloud[...].astype(F32).astype(BF16), jnp.where(in_block, 1.0, 0.0).astype(BF16))
    rows[...] = jnp.zeros_like(rows)
    rows[: WEEKS * NF, :] = forcing[...].astype(F32).reshape(WEEKS * NF, pixels)
    rows[OBS_AT : OBS_AT + WEEKS, :] = observed[...].astype(F32)
    rows[WGT_AT : WGT_AT + WEEKS, :] = seen / sigma[...].reshape(1, pixels)
    packed = nt(select, rows[...].astype(BF16))
    for c in range(n_crop):
        message[c] = packed[HALF * c : HALF * (c + 1), :]

    pl.semaphore_wait(barrier, 3 + n_crop - 1 + peers - 1 + jnp.where(inside, 4, 2))
    near_copies = [
        remote(near.at[x_at], near.at[x_at], near_send.at[k], near_recv.at[x_at], x_peer(k))
        for k in range(1, 4)
    ]
    for copy in near_copies:
        copy.start()
    copies = []
    for k in range(1, n_crop):
        where = crop_peer(k)
        copy = remote(message.at[where["crop"]], got.at[k], send.at[k], recv.at[k], where)
        copy.start()
        copies.append(copy)
    got[0] = message[crop]

    for copy in loads[6:]:
        copy.wait()
    mixes = [mix_weight[0, l] for l in range(3)]
    convs = [conv_weight[0, l] for l in range(3)]
    cur = [c[:, :CH] for c in convs]
    old = [c[:, CH:] for c in convs]
    head = head_weight[...]
    w_in = input_weight[0]
    cur_in = [nt(a, w_in) for a in cur]
    old_in = [nt(a, w_in) for a in old]
    head_in = nt(head, w_in)
    head_mix = [dot(head, m) for m in mixes]
    zero_row = jnp.zeros((1, CH), F32)
    for late in range(2):
        def outer(l):
            both = cur_in[l] + old_in[l] if late else cur_in[l]
            return [
                cur_in[l][:, :NF], old_in[l][:, :NF], both[:, NF:], jnp.zeros((CH, 8), F32)
            ]

        w1 = [dot(cur[1], mixes[0]), dot(old[1], mixes[0])]
        w1_hi, w1_lo = hi_lo(jnp.concatenate(w1 + outer(1), axis=1))
        w1_all[late, :CH] = w1_hi
        w1_all[late, CH:] = w1_lo
        w2 = [dot(a, m) for m in mixes[:2] for a in (cur[2], old[2])]
        w2_hi, w2_lo = hi_lo(jnp.concatenate(w2 + outer(2), axis=1))
        w2_all[late, :CH] = w2_hi
        w2_all[late, CH : 2 * CH] = w2_lo
        head2 = jnp.concatenate(
            [
                head_mix[0], zero_row, head_mix[1], zero_row,
                head_in[:, :NF], jnp.zeros((1, NF), F32), head_in[:, NF:],
                jnp.zeros((1, 8), F32),
            ],
            axis=1,
        )
        head2 = jnp.broadcast_to(head2, (16, 5 * CH))
        h2_hi = head2.astype(BF16).astype(F32)
        turn = iota((16, 5 * CH), 0)
        h2 = jnp.where(turn == 0, h2_hi, jnp.where(turn == 1, head2 - h2_hi, 0.0))
        w2_all[late, 2 * CH :] = h2.astype(BF16)
    last = jnp.transpose(jnp.broadcast_to(head_mix[2], (128, CH)))
    last = jnp.concatenate([last, last], axis=1)

    weight = jnp.concatenate([cur_in[0][:, :NF], old_in[0][:, :NF]], axis=1)
    hi = weight.astype(BF16).astype(F32)
    lf = jnp.concatenate([hi, weight - hi], axis=1).astype(BF16)

    def theta_weight(x):
        x = jnp.concatenate([x[:, NF:], jnp.zeros((x.shape[0], 8), F32)], axis=1)
        hi = x.astype(BF16).astype(F32)
        return jnp.concatenate([hi, x - hi], axis=1).astype(BF16)

    theta_weights = [theta_weight(cur_in[0]), theta_weight(cur_in[0] + old_in[0])]

    for k in range(1, 4):
        source = (x_at + k) % 4
        remote(
            near.at[source], near.at[source], near_send.at[k], near_recv.at[source], x_peer(k)
        ).wait_recv()
    merged[...] = (near[0] + near[1]) + (near[2] + near[3])

    def far_copy(k):
        where = far_target(k)[2]
        return remote(
            far_message.at[k], pars.at[z_high], far_send.at[k], far_recv.at[z_high], where
        )

    for k in range(4):
        wanted_region, wanted_crop, where = far_target(k)
        wanted_crop = wanted_crop % n_crop
        for a in range(MSUB):
            far_message[k, a, 0:1, :] = merged[a, pl.ds(wanted_region, 1), :]
            far_message[k, a, 1:2, :] = merged[a, pl.ds(wanted_crop, 1), :]
        if k < 2:
            far_copy(k).start()
        else:

            @pl.when(inside)
            def _():
                far_copy(k).start()

    for a in range(MSUB):
        pars[z_high, a, 0:1, :] = merged[a, pl.ds(region, 1), :]
        pars[z_high, a, 1:2, :] = merged[a, pl.ds(crop, 1), :]

    for copy in copies:
        copy.wait_recv()
    for a in range(MSUB):
        for k in range(SLOTS // HALF):
            at = a * SLOTS + k * HALF
            stacked[at : at + HALF, :] = got[k]
    ft[: PAD * NF, :] = jnp.zeros((PAD * NF, LANES), F32)
    ft[PAD * NF :, :] = jnp.transpose(stacked[...])

    def several(body, count):
        def step(i, carry):
            for d in range(count):
                body(i * count + d)
            return carry

        lax.fori_loop(0, WEEKS // count, step, 0)

    def forcing_rows(t, delay):
        now = ft[pl.ds((t + PAD) * NF, NF), :]
        late = ft[pl.ds((t + PAD - delay) * NF, NF), :]
        return jnp.concatenate([now, late], axis=0).astype(BF16)

    def forcing_part(t):
        x = forcing_rows(t, 1)
        fpart[t] = dot(lf, jnp.concatenate([x, x], axis=0))

    several(forcing_part, 13)
    inner0[:PAD] = jnp.zeros((PAD, CH, width), BF16)
    inner1[:PAD] = jnp.zeros((PAD, CH, width), BF16)

    for k in range(1, 4):
        high, where = far_source(k)
        remote(
            far_message.at[0], pars.at[high], far_send.at[0], far_recv.at[high], where
        ).wait_recv()
    for h in range(4):
        for a in range(MSUB):
            theta_rows[h * MSUB + a : h * MSUB + a + 1, :] = pars[h, a, 0:1, :]
    theta = theta_rows[...].astype(BF16)
    lane_of = iota((16, 512), 1) // SLOTS == iota((16, 512), 0)
    lane_of = jnp.where(lane_of, 1.0, 0.0).astype(BF16)
    theta_wide = jnp.concatenate(
        [tn(theta[:, 32 * q : 32 * (q + 1)], lane_of) for q in range(4)], axis=1
    )
    theta_all[...] = theta_wide.astype(BF16)
    theta_twice = jnp.concatenate([theta_wide, theta_wide], axis=0).astype(BF16)
    for l in range(2):
        gpart[l] = dot(theta_weights[l], theta_twice)

    def twice(x):
        return jnp.concatenate([x, x], axis=1)

    zero16 = jnp.zeros((CH, 256), BF16)

    def layer01(t):
        g0 = jnp.where(t >= 1, 1, 0)
        weight = w1_all[jnp.where(t >= 2, 1, 0)]
        f = twice(fpart[t])
        force = twice(forcing_rows(t, 2))
        for j in range(tiles):
            at = pl.ds(j * 256, 256)
            x0 = jnp.maximum((f + gpart[g0, :, at]).astype(BF16), zero16)
            inner0[t + PAD, :, at] = x0
            x = [x0, inner0[t + PAD - 2, :, at], force, theta_all[:, at]]
            y = dot(weight, jnp.concatenate(x, axis=0))
            y = y[:CH] + y[CH:]
            inner1[t + PAD, :, at] = jnp.maximum(y.astype(BF16), zero16)

    several(layer01, 13)

    def layer2(t):
        weight = w2_all[jnp.where(t >= 4, 1, 0)]
        force = twice(forcing_rows(t, 4))
        for j in range(tiles):
            at = pl.ds(j * 256, 256)
            x = jnp.concatenate(
                [
                    inner0[t + PAD, :, at],
                    inner0[t + PAD - 4, :, at],
                    inner1[t + PAD, :, at],
                    inner1[t + PAD - 4, :, at],
                    force,
                    theta_all[:, at],
                ],
                axis=0,
            )
            y = dot(weight, x)
            z = jnp.maximum(y[:CH] + y[CH : 2 * CH], 0.0) * last
            line = jnp.sum(z, axis=0, keepdims=True)
            line = line + y[2 * CH : 2 * CH + 1] + y[2 * CH + 1 : 2 * CH + 2]
            pred[t, 2 * j : 2 * j + 1, :] = line[:, :LANES]
            pred[t, 2 * j + 1 : 2 * j + 2, :] = line[:, LANES:]

    several(layer2, 13)

    p = pred[...]
    total = jnp.sum(p, axis=1)
    total = total + pltpu.roll(total, 2 * SLOTS, 1)
    total = total + pltpu.roll(total, SLOTS, 1)
    mean = total / members
    base = PAD * NF
    obs = ft[base + OBS_AT : base + OBS_AT + WEEKS, :]
    wgt = ft[base + WGT_AT : base + WGT_AT + WEEKS, :]
    innovation = wgt * (obs - mean) / math.sqrt(ALPHA_INFLATION)
    factor = wgt / math.sqrt(ALPHA_INFLATION * (members - 1))
    pred[...] = (p - mean[:, None, :]) * factor[:, None, :]

    block = iota((groups, LANES), 1) // SLOTS
    ext[members:, :] = jnp.zeros((ext.shape[0] - members, ext.shape[1]), BF16)
    block8 = iota((8, LANES), 1) // SLOTS
    row8 = iota((8, LANES), 0)
    for q in range(WEEKS // MSUB):
        weeks = [pred[MSUB * q + b] for b in range(MSUB)]
        parts = []
        for a in range(MSUB):
            turned = weeks[a]
            for b in range(MSUB):
                if b != a:
                    moved = pltpu.roll(weeks[b], (b - a) % MSUB * SLOTS, 1)
                    turned = jnp.where(block == b, moved, turned)
            parts.append(turned)
        cols = slice(LANES * q, LANES * (q + 1))
        ext[:members, cols] = jnp.concatenate(parts, axis=0).astype(BF16)
        inn = jnp.zeros((8, LANES), F32)
        for b in range(MSUB):
            line = jnp.broadcast_to(innovation[MSUB * q + b : MSUB * q + b + 1], (8, LANES))
            inn = jnp.where(block8 == b, line, inn)
        hi = inn.astype(BF16).astype(F32)
        inn = jnp.where(row8 == 0, hi, jnp.where(row8 == 1, inn - hi, 0.0))
        inn = jnp.concatenate([inn, jnp.zeros((8, LANES), F32)], axis=0)
        ext[members : members + 16, cols] = inn.astype(BF16)
    gram[...] = nt(ext[:members, :], ext[...]).reshape(n_crop, 8, 128)

    sums = []
    for k in range(1, n_crop):
        where = crop_peer(k)
        copy = remote(gram.at[where["crop"]], part.at[k], send_a.at[k], recv_a.at[k], where)
        copy.start()
        sums.append(copy)

    for h in range(4):
        for a in range(MSUB):
            theta_rows[h * MSUB + a : h * MSUB + a + 1, :] = pars[h, a, 1:2, :]
    theta = theta_rows[...]
    for q in range(4):
        turned = pltpu.roll(theta, (4 - q) % 4 * 32, 1) if q else theta
        for h in range(4):
            for a in range(MSUB):
                at = a * groups + q * 4 + h
                spread_rows[at : at + 1, :] = turned[h * MSUB + a : h * MSUB + a + 1, :]
    lane = iota((members, 128), 1)
    row = iota((members, 128), 0)
    theta = jnp.where(lane < NP, spread_rows[...], 0.0)
    centre = jnp.sum(theta, axis=0, keepdims=True) / members
    spread = (theta - centre) / math.sqrt(members - 1)

    acc = gram[crop]
    for copy in sums:
        copy.wait_recv()
    for k in range(1, n_crop):
        acc = acc + part[k]
    one[0] = acc
    adds = []
    for k in range(1, peers):
        q, where = sum_peer(k)
        copy = remote(one.at[0], every.at[mine], send_b.at[k], recv_b.at[mine], where)
        copy.start()
        adds.append(copy)
    every[mine] = acc
    for k in range(1, peers):
        q, where = sum_peer(k)
        remote(one.at[0], every.at[q], send_b.at[k], recv_b.at[q], where).wait_recv()
    acc = every[0]
    for q in range(1, peers):
        acc = acc + every[q]
    one[1] = acc

    beside = (x_at + jnp.where(half == 0, 3, 1)) % 4

    def row_copy(k):
        to_x = x_at if k < 4 else beside
        where = {"crop": region, "member": to_x * 4 + (z_high + k) % 4}
        return remote(one.at[1], final.at[crop], send_c.at[k], recv_c.at[crop], where)

    away = region != crop
    for k in (2, 6, 1, 3, 5, 7, 4):
        row_copy(k).start()

    @pl.when(away)
    def _():
        row_copy(0).start()

    @pl.when(jnp.logical_not(away))
    def _():
        final[crop] = one[1]

    from_x = jnp.where(x_at // 2 == crop % 2, x_at, beside)

    def row_arrival(source):
        where = {"crop": source, "member": from_x * 4 + crop // 2}
        return remote(one.at[1], final.at[source], send_c.at[0], recv_c.at[source], where)

    for k in range(1, n_crop):
        row_arrival((crop + k) % n_crop).wait_recv()

    @pl.when(away)
    def _():
        row_arrival(crop).wait_recv()

    whole = final[...].reshape(members, 128)
    proj = whole[:, members : members + 1] + whole[:, members + 1 : members + 2]
    moved = pltpu.roll(spread, members, 1)
    system = jnp.where(lane < members, whole + jnp.where(lane == row, 1.0, 0.0), moved)
    def wide(x):
        return jnp.broadcast_to(x, (1, 128))

    inverse = 1.0 / wide(system[0:1, 0:1])
    for k in range(members):
        line = system[k : k + 1]
        column = jnp.broadcast_to(system[:, k : k + 1], (members, 128))
        column = column - jnp.where(row == k, 1.0, 0.0)
        ahead = None
        if k + 1 < members:
            after = system[k + 1 : k + 2]
            pivot = wide(after[:, k : k + 1]) * (wide(line[:, k + 1 : k + 2]) * inverse)
            ahead = 1.0 / (wide(after[:, k + 1 : k + 2]) - pivot)
        system = system - column * (line * inverse)
        inverse = ahead
    y = jnp.where(lane >= members, system, 0.0)
    y = pltpu.roll(y, 128 - members, 1)
    solved[...] = y
    shared = centre + jnp.sum(proj * y, axis=0, keepdims=True)
    for a in range(MSUB):
        own = solved[pl.ds(a * groups + member, 1), :]
        result = shared + math.sqrt(members - 1) * own
        out[a] = result[:, :NP]

    for copy in near_copies + sums + adds:
        copy.wait_send()
    for copy in copies:
        copy.wait_send()
    for k in range(4):
        if k < 2:
            far_copy(k).wait_send()
        else:

            @pl.when(inside)
            def _():
                far_copy(k).wait_send()

    for k in range(1, 8):
        row_copy(k).wait_send()

    @pl.when(away)
    def _():
        row_copy(0).wait_send()


def local(
    sizes,
    forcing, observed, obs_sigma, pixel_class, pixel_count, cloud_free, params,
    input_weight, conv_weight, mix_weight, head_weight,
):
    n_pixel, n_crop, n_member = sizes
    pixels = obs_sigma.shape[0]
    members = params.shape[0] * n_member
    groups = members // MSUB
    width = groups * LANES
    args = (
        forcing, observed, obs_sigma, pixel_class.reshape(1, pixels), pixel_count, cloud_free,
        params, jnp.swapaxes(input_weight, 1, 2), conv_weight, mix_weight, head_weight,
    )
    anywhere = pl.BlockSpec(memory_space=pl.ANY)
    vmem = pl.BlockSpec(memory_space=pltpu.VMEM)
    smem = pl.BlockSpec(memory_space=pltpu.SMEM)
    dma = pltpu.SemaphoreType.DMA
    copies = [pltpu.VMEM(a.shape, a.dtype) for i, a in enumerate(args) if i != 4]
    return pl.pallas_call(
        functools.partial(mega_kernel, n_pixel, n_crop),
        name="smoother",
        out_shape=jax.ShapeDtypeStruct((MSUB, 1, NP), F32),
        in_specs=[smem if i == 4 else anywhere for i in range(len(args))],
        out_specs=vmem,
        scratch_shapes=copies + [
            pltpu.VMEM((ROW, pixels), F32),
            pltpu.VMEM((n_crop, HALF, ROW), F32),
            pltpu.VMEM((n_crop, HALF, ROW), F32),
            pltpu.VMEM((4, MSUB, 8, 128), F32),
            pltpu.VMEM((MSUB, 8, 128), F32),
            pltpu.VMEM((4, MSUB, 2, 128), F32),
            pltpu.VMEM((4, MSUB, 2, 128), F32),
            pltpu.VMEM((16, 128), F32),
            pltpu.VMEM((LANES, ROW), F32),
            pltpu.VMEM((PAD * NF + ROW, LANES), F32),
            pltpu.VMEM((WEEKS, CH, LANES), F32),
            pltpu.VMEM((2, CH, width), F32),
            pltpu.VMEM((32, width), BF16),
            pltpu.VMEM((2, 2 * CH, 3 * CH), BF16),
            pltpu.VMEM((2, 2 * CH + 16, 5 * CH), BF16),
            pltpu.VMEM((PAD + WEEKS, CH, width), BF16),
            pltpu.VMEM((PAD + WEEKS, CH, width), BF16),
            pltpu.VMEM((WEEKS, groups, LANES), F32),
            pltpu.VMEM((128, WEEKS // MSUB * LANES), BF16),
            pltpu.VMEM((n_crop, 8, 128), F32),
            pltpu.VMEM((n_crop, 8, 128), F32),
            pltpu.VMEM((2, 8, 128), F32),
            pltpu.VMEM((2 * n_pixel, 8, 128), F32),
            pltpu.VMEM((n_crop, 8, 128), F32),
            pltpu.VMEM((members, 128), F32),
            pltpu.VMEM((members, 128), F32),
            dma((10,)), dma((n_crop,)), dma((n_crop,)), dma((4,)), dma((4,)), dma((4,)), dma((4,)),
            dma((n_crop,)), dma((n_crop,)), dma((2 * n_pixel,)), dma((2 * n_pixel,)),
            dma((8,)), dma((n_crop,)),
        ],
        compiler_params=pltpu.CompilerParams(
            collective_id=0, has_side_effects=True, vmem_limit_bytes=(64 << 20) - 4096
        ),
    )(*args)


def solution(mesh):
    sizes = (mesh.shape["pixel"], mesh.shape["crop"], mesh.shape["member"])
    in_specs = (
        P(None, None, ("pixel", "crop")),
        P(None, ("pixel", "crop")),
        P(("pixel", "crop")),
        P(("pixel", "crop"), None),
        P(("pixel", "crop")),
        P(("pixel", "crop"), None),
        P("member", None, None),
        P("crop", None, None),
        P("crop", None, None, None),
        P("crop", None, None, None),
        P("crop", None),
    )
    return jax.shard_map(
        functools.partial(local, sizes),
        mesh=mesh,
        in_specs=in_specs,
        out_specs=P("member", "crop", None),
        check_vma=False,
    )
```

```python
import functools
import math

import jax
import jax.numpy as jnp
from jax import lax
from jax.experimental import pallas as pl
from jax.experimental.pallas import tpu as pltpu
from jax.sharding import PartitionSpec as P

MESH = pl.DeviceIdType.MESH
F32 = jnp.float32
BF16 = jnp.bfloat16
WEEKS = 52
CH = 48
NF = 8
NP = 24
CAP = 8
BLK = 32
ALPHA_INFLATION = 4.0
HALF = CAP // 2
SLOTS = 32
MSUB = 4
LANES = MSUB * SLOTS
ROW = 640
OBS_AT = 512
WGT_AT = 576
PAD = 4


def iota(shape, dim):
    return lax.broadcasted_iota(jnp.int32, shape, dim)


def nt(a, b):
    return lax.dot_general(a, b, (((1,), (1,)), ((), ())), preferred_element_type=F32)


def tn(a, b):
    return lax.dot_general(a, b, (((0,), (0,)), ((), ())), preferred_element_type=F32)


def hi_lo(x):
    hi = x.astype(BF16)
    return hi, (x - hi.astype(F32)).astype(BF16)


def mega_kernel(
    n_pixel, n_crop,
    forcing_hbm, observed_hbm, sigma_hbm, classes_hbm, counts, cloud_hbm, params_hbm,
    input_hbm, conv_hbm, mix_hbm, head_hbm,
    out,
    forcing, observed, sigma, classes, cloud, params, input_weight, conv_weight, mix_weight,
    head_weight,
    rows, message, got, near, merged, far_message, pars, theta_rows,
    stacked, ft, fpart, gpart, theta_all, w1_all, w2_all, inner0, inner1, pred, ext,
    gram, part, one, every, final, spread_rows, solved,
    load, send, recv, near_send, near_recv, far_send, far_recv,
    send_a, recv_a, send_b, recv_b, send_c, recv_c,
):
    pixel = lax.axis_index("pixel")
    crop = lax.axis_index("crop")
    member = lax.axis_index("member")
    x_at = member // 4
    z_high = member % 4
    z_low = crop // 2
    core = crop % 2
    region = z_high * 2 + x_at // 2
    half = x_at % 2
    pixels = rows.shape[1]
    blocks = cloud.shape[0]
    peers = 2 * n_pixel
    mine = pixel * 2 + half
    members = spread_rows.shape[0]
    groups = members // MSUB
    width = groups * LANES
    tiles = width // 256

    def dot(a, b):
        return jnp.dot(a, b, preferred_element_type=F32)

    def remote(src, dst, send_sem, recv_sem, where):
        return pltpu.make_async_remote_copy(
            src_ref=src, dst_ref=dst, send_sem=send_sem, recv_sem=recv_sem,
            device_id=where, device_id_type=MESH,
        )

    loads = []
    pairs = (
        (params_hbm, params), (forcing_hbm, forcing), (observed_hbm, observed),
        (sigma_hbm, sigma), (classes_hbm, classes), (cloud_hbm, cloud),
        (input_hbm, input_weight), (conv_hbm, conv_weight), (mix_hbm, mix_weight),
        (head_hbm, head_weight),
    )
    for i, (src, dst) in enumerate(pairs):
        copy = pltpu.make_async_copy(src, dst, load.at[i])
        copy.start()
        loads.append(copy)

    def crop_peer(k):
        return {"crop": (crop + k) % n_crop}

    def x_peer(k):
        return {"member": (x_at + k) % 4 * 4 + z_high}

    def sum_peer(k):
        q = (mine + k) % peers
        return q, {"pixel": q // 2, "member": (x_at // 2 * 2 + q % 2) * 4 + z_high}

    inside = (z_low == 1) | (z_low == 2)
    slab = jnp.where(z_low == 2, 1, jnp.where(z_low == 1, 3, 2))

    def far_target(k):
        z_to = k + jnp.where(z_low == 0, 2, 0)
        high = (z_high + slab) % 4
        return high * 2 + x_at // 2, z_to * 2 + core, {
            "crop": z_to * 2 + core, "member": x_at * 4 + high
        }

    def far_source(k):
        z_from = (1, jnp.where(z_low < 2, 3, 0), 2)[k - 1]
        high = (z_high + k) % 4
        return high, {"crop": z_from * 2 + core, "member": x_at * 4 + high}

    barrier = pltpu.get_barrier_semaphore()
    for k in range(1, 4):
        pl.semaphore_signal(barrier, inc=1, device_id=far_source(k)[1], device_id_type=MESH)
    for k in range(1, n_crop):
        pl.semaphore_signal(barrier, inc=1, device_id=crop_peer(k), device_id_type=MESH)
    for k in range(1, 4):
        pl.semaphore_signal(barrier, inc=1, device_id=x_peer(k), device_id_type=MESH)
    for k in range(1, peers):
        pl.semaphore_signal(barrier, inc=1, device_id=sum_peer(k)[1], device_id_type=MESH)

    loads[0].wait()
    quarter = iota((8, 128), 1) // 32
    for a in range(MSUB):
        block = jnp.concatenate([params[a], jnp.zeros((8, 32 - NP), F32)], axis=1)
        block = jnp.concatenate([block] * 4, axis=1)
        near[x_at, a] = jnp.where(quarter == x_at, block, 0.0)

    for copy in loads[1:6]:
        copy.wait()
    place = iota((1, pixels), 1)
    limit = jnp.zeros((1, pixels), jnp.int32)
    for b in range(blocks):
        limit = jnp.where(place // BLK == b, counts[b], limit)
    live = place % BLK < limit
    slots = n_crop * HALF
    slot = iota((slots, pixels), 0)
    named = (classes[...] == (slot // HALF) * 8 + region) & live
    named = jnp.where(named, 1.0, 0.0)
    before = jnp.where(iota((pixels, pixels), 0) < iota((pixels, pixels), 1), 1.0, 0.0)
    rank = dot(named.astype(BF16), before.astype(BF16))
    wanted = (slot % HALF + half * HALF).astype(F32)
    select = jnp.where(rank == wanted, named, 0.0).astype(BF16)

    in_block = iota((blocks, pixels), 1) // BLK == iota((blocks, pixels), 0)
    seen = tn(cloud[...].astype(F32).astype(BF16), jnp.where(in_block, 1.0, 0.0).astype(BF16))
    rows[...] = jnp.zeros_like(rows)
    rows[: WEEKS * NF, :] = forcing[...].astype(F32).reshape(WEEKS * NF, pixels)
    rows[OBS_AT : OBS_AT + WEEKS, :] = observed[...].astype(F32)
    rows[WGT_AT : WGT_AT + WEEKS, :] = seen / sigma[...].reshape(1, pixels)
    packed = nt(select, rows[...].astype(BF16))
    for c in range(n_crop):
        message[c] = packed[HALF * c : HALF * (c + 1), :]

    pl.semaphore_wait(barrier, 3 + n_crop - 1 + peers - 1 + jnp.where(inside, 4, 2))
    near_copies = [
        remote(near.at[x_at], near.at[x_at], near_send.at[k], near_recv.at[x_at], x_peer(k))
        for k in range(1, 4)
    ]
    for copy in near_copies:
        copy.start()
    copies = []
    for k in range(1, n_crop):
        where = crop_peer(k)
        copy = remote(message.at[where["crop"]], got.at[k], send.at[k], recv.at[k], where)
        copy.start()
        copies.append(copy)
    got[0] = message[crop]

    for k in range(1, 4):
        source = (x_at + k) % 4
        remote(
            near.at[source], near.at[source], near_send.at[k], near_recv.at[source], x_peer(k)
        ).wait_recv()
    merged[...] = (near[0] + near[1]) + (near[2] + near[3])

    def far_copy(k):
        where = far_target(k)[2]
        return remote(
            far_message.at[k], pars.at[z_high], far_send.at[k], far_recv.at[z_high], where
        )

    for k in range(4):
        wanted_region, wanted_crop, where = far_target(k)
        wanted_crop = wanted_crop % n_crop
        for a in range(MSUB):
            far_message[k, a, 0:1, :] = merged[a, pl.ds(wanted_region, 1), :]
            far_message[k, a, 1:2, :] = merged[a, pl.ds(wanted_crop, 1), :]
        if k < 2:
            far_copy(k).start()
        else:

            @pl.when(inside)
            def _():
                far_copy(k).start()

    for a in range(MSUB):
        pars[z_high, a, 0:1, :] = merged[a, pl.ds(region, 1), :]
        pars[z_high, a, 1:2, :] = merged[a, pl.ds(crop, 1), :]

    for copy in loads[6:]:
        copy.wait()
    mixes = [mix_weight[0, l] for l in range(3)]
    convs = [conv_weight[0, l] for l in range(3)]
    cur = [c[:, :CH] for c in convs]
    old = [c[:, CH:] for c in convs]
    head = head_weight[...]
    w_in = input_weight[0]
    cur_in = [nt(a, w_in) for a in cur]
    old_in = [nt(a, w_in) for a in old]
    head_in = nt(head, w_in)
    head_mix = [dot(head, m) for m in mixes]
    zero_row = jnp.zeros((1, CH), F32)
    for late in range(2):
        def outer(l):
            both = cur_in[l] + old_in[l] if late else cur_in[l]
            return [
                cur_in[l][:, :NF], old_in[l][:, :NF], both[:, NF:], jnp.zeros((CH, 8), F32)
            ]

        w1 = [dot(cur[1], mixes[0]), dot(old[1], mixes[0])]
        w1_hi, w1_lo = hi_lo(jnp.concatenate(w1 + outer(1), axis=1))
        w1_all[late, :CH] = w1_hi
        w1_all[late, CH:] = w1_lo
        w2 = [dot(a, m) for m in mixes[:2] for a in (cur[2], old[2])]
        w2_hi, w2_lo = hi_lo(jnp.concatenate(w2 + outer(2), axis=1))
        w2_all[late, :CH] = w2_hi
        w2_all[late, CH : 2 * CH] = w2_lo
        head2 = jnp.concatenate(
            [
                head_mix[0], zero_row, head_mix[1], zero_row,
                head_in[:, :NF], jnp.zeros((1, NF), F32), head_in[:, NF:],
                jnp.zeros((1, 8), F32),
            ],
            axis=1,
        )
        head2 = jnp.broadcast_to(head2, (16, 5 * CH))
        h2_hi = head2.astype(BF16).astype(F32)
        turn = iota((16, 5 * CH), 0)
        h2 = jnp.where(turn == 0, h2_hi, jnp.where(turn == 1, head2 - h2_hi, 0.0))
        w2_all[late, 2 * CH :] = h2.astype(BF16)
    last = jnp.transpose(jnp.broadcast_to(head_mix[2], (128, CH)))
    last = jnp.concatenate([last, last], axis=1)

    weight = jnp.concatenate([cur_in[0][:, :NF], old_in[0][:, :NF]], axis=1)
    hi = weight.astype(BF16).astype(F32)
    lf = jnp.concatenate([hi, weight - hi], axis=1).astype(BF16)

    def theta_weight(x):
        x = jnp.concatenate([x[:, NF:], jnp.zeros((x.shape[0], 8), F32)], axis=1)
        hi = x.astype(BF16).astype(F32)
        return jnp.concatenate([hi, x - hi], axis=1).astype(BF16)

    theta_weights = [theta_weight(cur_in[0]), theta_weight(cur_in[0] + old_in[0])]

    for copy in copies:
        copy.wait_recv()
    for a in range(MSUB):
        for k in range(SLOTS // HALF):
            at = a * SLOTS + k * HALF
            stacked[at : at + HALF, :] = got[k]
    ft[: PAD * NF, :] = jnp.zeros((PAD * NF, LANES), F32)
    ft[PAD * NF :, :] = jnp.transpose(stacked[...])

    def several(body, count):
        def step(i, carry):
            for d in range(count):
                body(i * count + d)
            return carry

        lax.fori_loop(0, WEEKS // count, step, 0)

    def forcing_rows(t, delay):
        now = ft[pl.ds((t + PAD) * NF, NF), :]
        late = ft[pl.ds((t + PAD - delay) * NF, NF), :]
        return jnp.concatenate([now, late], axis=0).astype(BF16)

    def forcing_part(t):
        x = forcing_rows(t, 1)
        fpart[t] = dot(lf, jnp.concatenate([x, x], axis=0))

    several(forcing_part, 13)
    inner0[:PAD] = jnp.zeros((PAD, CH, width), BF16)
    inner1[:PAD] = jnp.zeros((PAD, CH, width), BF16)

    for k in range(1, 4):
        high, where = far_source(k)
        remote(
            far_message.at[0], pars.at[high], far_send.at[0], far_recv.at[high], where
        ).wait_recv()
    for h in range(4):
        for a in range(MSUB):
            theta_rows[h * MSUB + a : h * MSUB + a + 1, :] = pars[h, a, 0:1, :]
    theta = theta_rows[...].astype(BF16)
    lane_of = iota((16, 512), 1) // SLOTS == iota((16, 512), 0)
    lane_of = jnp.where(lane_of, 1.0, 0.0).astype(BF16)
    theta_wide = jnp.concatenate(
        [tn(theta[:, 32 * q : 32 * (q + 1)], lane_of) for q in range(4)], axis=1
    )
    theta_all[...] = theta_wide.astype(BF16)
    theta_twice = jnp.concatenate([theta_wide, theta_wide], axis=0).astype(BF16)
    for l in range(2):
        gpart[l] = dot(theta_weights[l], theta_twice)

    def twice(x):
        return jnp.concatenate([x, x], axis=1)

    zero16 = jnp.zeros((CH, 256), BF16)

    def layer01(t):
        g0 = jnp.where(t >= 1, 1, 0)
        weight = w1_all[jnp.where(t >= 2, 1, 0)]
        f = twice(fpart[t])
        force = twice(forcing_rows(t, 2))
        for j in range(tiles):
            at = pl.ds(j * 256, 256)
            x0 = jnp.maximum((f + gpart[g0, :, at]).astype(BF16), zero16)
            inner0[t + PAD, :, at] = x0
            x = [x0, inner0[t + PAD - 2, :, at], force, theta_all[:, at]]
            y = dot(weight, jnp.concatenate(x, axis=0))
            y = y[:CH] + y[CH:]
            inner1[t + PAD, :, at] = jnp.maximum(y.astype(BF16), zero16)

    several(layer01, 26)

    def layer2(t):
        weight = w2_all[jnp.where(t >= 4, 1, 0)]
        force = twice(forcing_rows(t, 4))
        for j in range(tiles):
            at = pl.ds(j * 256, 256)
            x = jnp.concatenate(
                [
                    inner0[t + PAD, :, at],
                    inner0[t + PAD - 4, :, at],
                    inner1[t + PAD, :, at],
                    inner1[t + PAD - 4, :, at],
                    force,
                    theta_all[:, at],
                ],
                axis=0,
            )
            y = dot(weight, x)
            z = jnp.maximum(y[:CH] + y[CH : 2 * CH], 0.0) * last
            z = jnp.sum(z.reshape(CH // 8, 8, 256), axis=0) + y[2 * CH : 2 * CH + 8]
            line = jnp.sum(z, axis=0, keepdims=True)
            pred[t, 2 * j : 2 * j + 1, :] = line[:, :LANES]
            pred[t, 2 * j + 1 : 2 * j + 2, :] = line[:, LANES:]

    several(layer2, 26)

    p = pred[...]
    total = jnp.sum(p, axis=1)
    total = total + pltpu.roll(total, 2 * SLOTS, 1)
    total = total + pltpu.roll(total, SLOTS, 1)
    mean = total / members
    base = PAD * NF
    obs = ft[base + OBS_AT : base + OBS_AT + WEEKS, :]
    wgt = ft[base + WGT_AT : base + WGT_AT + WEEKS, :]
    innovation = wgt * (obs - mean) / math.sqrt(ALPHA_INFLATION)
    factor = wgt / math.sqrt(ALPHA_INFLATION * (members - 1))
    pred[...] = (p - mean[:, None, :]) * factor[:, None, :]

    block = iota((groups, LANES), 1) // SLOTS
    ext[members:, :] = jnp.zeros((ext.shape[0] - members, ext.shape[1]), BF16)
    block8 = iota((8, LANES), 1) // SLOTS
    row8 = iota((8, LANES), 0)
    for q in range(WEEKS // MSUB):
        weeks = [pred[MSUB * q + b] for b in range(MSUB)]
        parts = []
        for a in range(MSUB):
            turned = weeks[a]
            for b in range(MSUB):
                if b != a:
                    moved = pltpu.roll(weeks[b], (b - a) % MSUB * SLOTS, 1)
                    turned = jnp.where(block == b, moved, turned)
            parts.append(turned)
        cols = slice(LANES * q, LANES * (q + 1))
        ext[:members, cols] = jnp.concatenate(parts, axis=0).astype(BF16)
        inn = jnp.zeros((8, LANES), F32)
        for b in range(MSUB):
            line = jnp.broadcast_to(innovation[MSUB * q + b : MSUB * q + b + 1], (8, LANES))
            inn = jnp.where(block8 == b, line, inn)
        hi = inn.astype(BF16).astype(F32)
        inn = jnp.where(row8 == 0, hi, jnp.where(row8 == 1, inn - hi, 0.0))
        inn = jnp.concatenate([inn, jnp.zeros((8, LANES), F32)], axis=0)
        ext[members : members + 16, cols] = inn.astype(BF16)
    gram[...] = nt(ext[:members, :], ext[...]).reshape(n_crop, 8, 128)

    sums = []
    for k in range(1, n_crop):
        where = crop_peer(k)
        copy = remote(gram.at[where["crop"]], part.at[k], send_a.at[k], recv_a.at[k], where)
        copy.start()
        sums.append(copy)

    for h in range(4):
        for a in range(MSUB):
            theta_rows[h * MSUB + a : h * MSUB + a + 1, :] = pars[h, a, 1:2, :]
    theta = theta_rows[...]
    for q in range(4):
        turned = pltpu.roll(theta, (4 - q) % 4 * 32, 1) if q else theta
        for h in range(4):
            for a in range(MSUB):
                at = a * groups + q * 4 + h
                spread_rows[at : at + 1, :] = turned[h * MSUB + a : h * MSUB + a + 1, :]
    lane = iota((members, 128), 1)
    row = iota((members, 128), 0)
    theta = jnp.where(lane < NP, spread_rows[...], 0.0)
    centre = jnp.sum(theta, axis=0, keepdims=True) / members
    spread = (theta - centre) / math.sqrt(members - 1)

    acc = gram[crop]
    for copy in sums:
        copy.wait_recv()
    for k in range(1, n_crop):
        acc = acc + part[k]
    one[0] = acc
    adds = []
    for k in range(1, peers):
        q, where = sum_peer(k)
        copy = remote(one.at[0], every.at[mine], send_b.at[k], recv_b.at[mine], where)
        copy.start()
        adds.append(copy)
    every[mine] = acc
    for k in range(1, peers):
        q, where = sum_peer(k)
        remote(one.at[0], every.at[q], send_b.at[k], recv_b.at[q], where).wait_recv()
    acc = every[0]
    for q in range(1, peers):
        acc = acc + every[q]
    one[1] = acc

    beside = (x_at + jnp.where(half == 0, 3, 1)) % 4

    def row_copy(k):
        to_x = x_at if k < 4 else beside
        where = {"crop": region, "member": to_x * 4 + (z_high + k) % 4}
        return remote(one.at[1], final.at[crop], send_c.at[k], recv_c.at[crop], where)

    away = region != crop
    for k in (2, 6, 1, 3, 5, 7, 4):
        row_copy(k).start()

    @pl.when(away)
    def _():
        row_copy(0).start()

    @pl.when(jnp.logical_not(away))
    def _():
        final[crop] = one[1]

    from_x = jnp.where(x_at // 2 == crop % 2, x_at, beside)

    def row_arrival(source):
        where = {"crop": source, "member": from_x * 4 + crop // 2}
        return remote(one.at[1], final.at[source], send_c.at[0], recv_c.at[source], where)

    for k in range(1, n_crop):
        row_arrival((crop + k) % n_crop).wait_recv()

    @pl.when(away)
    def _():
        row_arrival(crop).wait_recv()

    whole = final[...].reshape(members, 128)
    proj = whole[:, members : members + 1] + whole[:, members + 1 : members + 2]
    moved = pltpu.roll(spread, members, 1)
    system = jnp.where(lane < members, whole + jnp.where(lane == row, 1.0, 0.0), moved)
    def wide(x):
        return jnp.broadcast_to(x, (1, 128))

    inverse = 1.0 / wide(system[0:1, 0:1])
    for k in range(members):
        line = system[k : k + 1]
        column = jnp.broadcast_to(system[:, k : k + 1], (members, 128))
        column = column - jnp.where(row == k, 1.0, 0.0)
        ahead = None
        if k + 1 < members:
            after = system[k + 1 : k + 2]
            pivot = wide(after[:, k : k + 1]) * (wide(line[:, k + 1 : k + 2]) * inverse)
            ahead = 1.0 / (wide(after[:, k + 1 : k + 2]) - pivot)
        system = system - column * (line * inverse)
        inverse = ahead
    y = jnp.where(lane >= members, system, 0.0)
    y = pltpu.roll(y, 128 - members, 1)
    solved[...] = y
    shared = centre + jnp.sum(proj * y, axis=0, keepdims=True)
    for a in range(MSUB):
        own = solved[pl.ds(a * groups + member, 1), :]
        result = shared + math.sqrt(members - 1) * own
        out[a] = result[:, :NP]

    for copy in near_copies + sums + adds:
        copy.wait_send()
    for copy in copies:
        copy.wait_send()
    for k in range(4):
        if k < 2:
            far_copy(k).wait_send()
        else:

            @pl.when(inside)
            def _():
                far_copy(k).wait_send()

    for k in range(1, 8):
        row_copy(k).wait_send()

    @pl.when(away)
    def _():
        row_copy(0).wait_send()


def local(
    sizes,
    forcing, observed, obs_sigma, pixel_class, pixel_count, cloud_free, params,
    input_weight, conv_weight, mix_weight, head_weight,
):
    n_pixel, n_crop, n_member = sizes
    pixels = obs_sigma.shape[0]
    members = params.shape[0] * n_member
    groups = members // MSUB
    width = groups * LANES
    args = (
        forcing, observed, obs_sigma, pixel_class.reshape(1, pixels), pixel_count, cloud_free,
        params, jnp.swapaxes(input_weight, 1, 2), conv_weight, mix_weight, head_weight,
    )
    anywhere = pl.BlockSpec(memory_space=pl.ANY)
    vmem = pl.BlockSpec(memory_space=pltpu.VMEM)
    smem = pl.BlockSpec(memory_space=pltpu.SMEM)
    dma = pltpu.SemaphoreType.DMA
    copies = [pltpu.VMEM(a.shape, a.dtype) for i, a in enumerate(args) if i != 4]
    return pl.pallas_call(
        functools.partial(mega_kernel, n_pixel, n_crop),
        name="smoother",
        out_shape=jax.ShapeDtypeStruct((MSUB, 1, NP), F32),
        in_specs=[smem if i == 4 else anywhere for i in range(len(args))],
        out_specs=vmem,
        scratch_shapes=copies + [
            pltpu.VMEM((ROW, pixels), F32),
            pltpu.VMEM((n_crop, HALF, ROW), F32),
            pltpu.VMEM((n_crop, HALF, ROW), F32),
            pltpu.VMEM((4, MSUB, 8, 128), F32),
            pltpu.VMEM((MSUB, 8, 128), F32),
            pltpu.VMEM((4, MSUB, 2, 128), F32),
            pltpu.VMEM((4, MSUB, 2, 128), F32),
            pltpu.VMEM((16, 128), F32),
            pltpu.VMEM((LANES, ROW), F32),
            pltpu.VMEM((PAD * NF + ROW, LANES), F32),
            pltpu.VMEM((WEEKS, CH, LANES), F32),
            pltpu.VMEM((2, CH, width), F32),
            pltpu.VMEM((32, width), BF16),
            pltpu.VMEM((2, 2 * CH, 3 * CH), BF16),
            pltpu.VMEM((2, 2 * CH + 16, 5 * CH), BF16),
            pltpu.VMEM((PAD + WEEKS, CH, width), BF16),
            pltpu.VMEM((PAD + WEEKS, CH, width), BF16),
            pltpu.VMEM((WEEKS, groups, LANES), F32),
            pltpu.VMEM((128, WEEKS // MSUB * LANES), BF16),
            pltpu.VMEM((n_crop, 8, 128), F32),
            pltpu.VMEM((n_crop, 8, 128), F32),
            pltpu.VMEM((2, 8, 128), F32),
            pltpu.VMEM((2 * n_pixel, 8, 128), F32),
            pltpu.VMEM((n_crop, 8, 128), F32),
            pltpu.VMEM((members, 128), F32),
            pltpu.VMEM((members, 128), F32),
            dma((10,)), dma((n_crop,)), dma((n_crop,)), dma((4,)), dma((4,)), dma((4,)), dma((4,)),
            dma((n_crop,)), dma((n_crop,)), dma((2 * n_pixel,)), dma((2 * n_pixel,)),
            dma((8,)), dma((n_crop,)),
        ],
        compiler_params=pltpu.CompilerParams(
            collective_id=0, has_side_effects=True, vmem_limit_bytes=(64 << 20) - 4096
        ),
    )(*args)


def solution(mesh):
    sizes = (mesh.shape["pixel"], mesh.shape["crop"], mesh.shape["member"])
    in_specs = (
        P(None, None, ("pixel", "crop")),
        P(None, ("pixel", "crop")),
        P(("pixel", "crop")),
        P(("pixel", "crop"), None),
        P(("pixel", "crop")),
        P(("pixel", "crop"), None),
        P("member", None, None),
        P("crop", None, None),
        P("crop", None, None, None),
        P("crop", None, None, None),
        P("crop", None),
    )
    return jax.shard_map(
        functools.partial(local, sizes),
        mesh=mesh,
        in_specs=in_specs,
        out_specs=P("member", "crop", None),
        check_vma=False,
    )
```
